256 devices in a mesh: ha: 16 (over x, y_hi, core), wa: 16 (over z, y_lo).
Axes of the slice: x: 4, y: 4 (y_hi: 2, y_lo: 2; y = y_hi * 2 + y_lo), z: 8, core: 2. Of those that a mesh axis runs over, the one named last changes fastest.
Arguments:
- tokens: bfloat16 [256, 256, 256], P('ha', 'wa'), may hold values from -6 to 6
- gain_attn: float32 [256], replicated, may hold values from 0.25 to 1.75
- qkv_fine: bfloat16 [256, 768], replicated, may hold values from -0.375 to 0.375
- scale_fine: float32 [4], replicated, may hold values from 2 to 24
- out_fine: bfloat16 [256, 256], replicated, may hold values from -0.375 to 0.375
- gain_ffn: float32 [256], replicated, may hold values from 0.25 to 1.75
- ffn_in: bfloat16 [256, 1536], replicated, may hold values from -0.375 to 0.375
- ffn_out: bfloat16 [768, 256], replicated, may hold values from -0.21875 to 0.21875
- up_proj: bfloat16 [256, 1024], replicated, may hold values from -0.375 to 0.375
- gain_coarse: float32 [1024], replicated, may hold values from 0.25 to 1.75
- qkv_coarse: bfloat16 [1024, 3072], replicated, may hold values from -0.1875 to 0.1875
- scale_coarse: float32 [16], replicated, may hold values from 2 to 24
- out_coarse: bfloat16 [1024, 1024], replicated, may hold values from -0.1875 to 0.1875
Outputs:
- fine_out: bfloat16 [256, 256, 256], P('ha', 'wa')
- coarse_out: bfloat16 [16, 16, 1024], P('ha', 'wa')
The draws below stay inside these ranges and needn't reach their ends.
All inputs are finite; a program needn't handle non-finite values.
Results may differ from the reference program's by a relative error of at most 0.03.
Values may be sent and summed in bfloat16 or wider, within the bound.
A program may use at most 128 MiB of HBM per device.

```python
import math
import jax
import jax.numpy as jnp
from jax import lax

C = 256
CC = 1024
HD = 64
FFH = 768
RADIUS = 3
POOL = 16
HEADS = 4
HEADS_C = 16
H0 = 256
W0 = 256


def block_levels(stream_key, shape, shards, least, largest):
    level, own = 1.0, jax.random.fold_in(stream_key, 6)
    for dim, parts in shards:
        draws = jnp.exp(jax.random.uniform(jax.random.fold_in(own, dim), (parts,), jnp.float32, least / len(shards), largest / len(shards)))
        level = level * jnp.repeat(draws, shape[dim] // parts).reshape([-1 if axis == dim else 1 for axis in range(len(shape))])
    return level


def centred(stream_key, shape, scale, most, pieces=(), kind=jnp.bfloat16):
    array = jax.random.normal(stream_key, shape, jnp.float32) * scale
    if len(pieces) > 0:
        array = block_levels(stream_key, shape, pieces, -0.22, 0.18) * array
    return jnp.clip(array, min=-most, max=most).astype(kind)


def setup_inputs(seed: int = 0) -> dict:
    arg_keys = jax.random.split(jax.random.key(seed), 14)
    tokens = centred(arg_keys[0], (H0, W0, C), 1.0, 6.0, ((0, 16), (1, 16)))
    gain_attn = jnp.clip(1.0 + 0.15 * jax.random.normal(arg_keys[1], (C,), jnp.float32), 0.25, 1.75)
    qkv_fine = centred(arg_keys[2], (C, 3 * C), C ** -0.5, 0.375)
    scale_fine = jnp.clip(jnp.exp(jax.random.uniform(arg_keys[3], (HEADS,), jnp.float32, math.log(2.0), math.log(24.0))), 2.0, 24.0)
    out_fine = centred(arg_keys[4], (C, C), C ** -0.5, 0.375)
    gain_ffn = jnp.clip(1.0 + 0.15 * jax.random.normal(arg_keys[5], (C,), jnp.float32), 0.25, 1.75)
    ffn_in = centred(arg_keys[6], (C, 2 * FFH), C ** -0.5, 0.375)
    ffn_out = centred(arg_keys[7], (FFH, C), FFH ** -0.5, 0.21875)
    up_proj = centred(arg_keys[8], (C, CC), C ** -0.5, 0.375)
    gain_coarse = jnp.clip(1.0 + 0.15 * jax.random.normal(arg_keys[9], (CC,), jnp.float32), 0.25, 1.75)
    qkv_coarse = centred(arg_keys[10], (CC, 3 * CC), CC ** -0.5, 0.1875)
    scale_coarse = jnp.clip(jnp.exp(jax.random.uniform(arg_keys[11], (HEADS_C,), jnp.float32, math.log(2.0), math.log(24.0))), 2.0, 24.0)
    out_coarse = centred(arg_keys[12], (CC, CC), CC ** -0.5, 0.1875)
    return dict(tokens=tokens, gain_attn=gain_attn, qkv_fine=qkv_fine, scale_fine=scale_fine, out_fine=out_fine, gain_ffn=gain_ffn, ffn_in=ffn_in, ffn_out=ffn_out, up_proj=up_proj, gain_coarse=gain_coarse, qkv_coarse=qkv_coarse, scale_coarse=scale_coarse, out_coarse=out_coarse)


def rms_scale(values, gain):
    values = values.astype(jnp.float32)
    return values * lax.rsqrt(lax.optimization_barrier(jnp.mean(values * values, -1, keepdims=True)) + 1e-06) * gain

def head_norm(values, heads):
    shaped = values.reshape(values.shape[:-1] + (heads, HD))
    return shaped * lax.rsqrt(lax.optimization_barrier(jnp.mean(shaped * shaped, -1, keepdims=True)) + 1e-06)

def reference(tokens, gain_attn, qkv_fine, scale_fine, out_fine, gain_ffn, ffn_in, ffn_out, up_proj, gain_coarse, qkv_coarse, scale_coarse, out_coarse):
    height, width_grid = (tokens.shape[0], tokens.shape[1])
    heads = C // HD
    count = height * width_grid
    normed = rms_scale(tokens, gain_attn).astype(jnp.bfloat16).reshape(count, C)
    proj = jnp.dot(normed, qkv_fine, preferred_element_type=jnp.float32).reshape(height, width_grid, 3 * C)
    query = head_norm(proj[..., :C], heads).astype(jnp.bfloat16).astype(jnp.float32)
    key = head_norm(proj[..., C:2 * C], heads).astype(jnp.bfloat16).astype(jnp.float32)
    value = proj[..., 2 * C:].reshape(height, width_grid, heads, HD).astype(jnp.bfloat16).astype(jnp.float32)
    pad_spec = ((RADIUS, RADIUS), (RADIUS, RADIUS), (0, 0), (0, 0))
    key_pad = jnp.pad(key, pad_spec)
    value_pad = jnp.pad(value, pad_spec)
    valid = jnp.pad(jnp.ones((height, width_grid), jnp.float32), RADIUS)
    span = 2 * RADIUS + 1
    score_list = []
    for shift_a in range(span):
        for shift_b in range(span):
            ks = key_pad[shift_a:shift_a + height, shift_b:shift_b + width_grid]
            inside = valid[shift_a:shift_a + height, shift_b:shift_b + width_grid]
            raw = jnp.einsum('xyhd,xyhd->xyh', query, ks) * scale_fine / HD
            score_list.append(jnp.where(inside[..., None] > 0.5, raw, -1e+30))
    scores = jnp.stack(score_list)
    top = lax.optimization_barrier(jnp.max(scores, 0, keepdims=True))
    expo = jnp.exp(scores - top)
    weights = (expo / lax.optimization_barrier(jnp.sum(expo, 0, keepdims=True))).astype(jnp.bfloat16).astype(jnp.float32)
    attn = jnp.zeros((height, width_grid, heads, HD), jnp.float32)
    index = 0
    for shift_a in range(span):
        for shift_b in range(span):
            vs = value_pad[shift_a:shift_a + height, shift_b:shift_b + width_grid]
            attn = attn + weights[index][..., None] * vs
            index = index + 1
    attn = attn.astype(jnp.bfloat16).reshape(count, C)
    h1 = (tokens.reshape(count, C).astype(jnp.float32) + jnp.dot(attn, out_fine, preferred_element_type=jnp.float32)).astype(jnp.bfloat16)
    n2 = rms_scale(h1, gain_ffn).astype(jnp.bfloat16)
    mixed = jnp.dot(n2, ffn_in, preferred_element_type=jnp.float32)
    gated = (jax.nn.gelu(mixed[:, :FFH], approximate=True) * mixed[:, FFH:]).astype(jnp.bfloat16)
    fine_out = (h1.astype(jnp.float32) + jnp.dot(gated, ffn_out, preferred_element_type=jnp.float32)).astype(jnp.bfloat16)
    fine_out = fine_out.reshape(height, width_grid, C)
    rows_c, cols_c = (height // POOL, width_grid // POOL)
    pooled = fine_out.astype(jnp.float32).reshape(rows_c, POOL, cols_c, POOL, C).mean(axis=(1, 3))
    pooled = pooled.astype(jnp.bfloat16).reshape(rows_c * cols_c, C)
    coarse = jnp.dot(pooled, up_proj, preferred_element_type=jnp.float32).astype(jnp.bfloat16)
    heads_c = CC // HD
    ncoarse = rms_scale(coarse, gain_coarse).astype(jnp.bfloat16)
    pc = jnp.dot(ncoarse, qkv_coarse, preferred_element_type=jnp.float32)
    cq = head_norm(pc[:, :CC], heads_c).astype(jnp.bfloat16).astype(jnp.float32)
    ck = head_norm(pc[:, CC:2 * CC], heads_c).astype(jnp.bfloat16).astype(jnp.float32)
    cv = pc[:, 2 * CC:].reshape(-1, heads_c, HD).astype(jnp.bfloat16).astype(jnp.float32)
    cscores = jnp.einsum('qhd,khd->hqk', cq, ck) * (scale_coarse / HD)[:, None, None]
    ctop = lax.optimization_barrier(jnp.max(cscores, -1, keepdims=True))
    cexp = jnp.exp(cscores - ctop)
    cweights = (cexp / lax.optimization_barrier(jnp.sum(cexp, -1, keepdims=True))).astype(jnp.bfloat16).astype(jnp.float32)
    cattn = jnp.einsum('hqk,khd->qhd', cweights, cv).astype(jnp.bfloat16).reshape(-1, CC)
    coarse_out = (coarse.astype(jnp.float32) + jnp.dot(cattn, out_coarse, preferred_element_type=jnp.float32)).astype(jnp.bfloat16)
    return (fine_out, coarse_out.reshape(rows_c, cols_c, CC))
```

```python
import functools

import jax
import jax.numpy as jnp
import numpy as np
from jax import lax
from jax.experimental import pallas as pl
from jax.experimental.pallas import tpu as pltpu
from jax.sharding import PartitionSpec as P

C = 256
CC = 1024
HD = 64
FFH = 768
RADIUS = 3
SIDE = 16
COUNT = SIDE * SIDE
HEADS = 4
HEADS_C = 16
EPS = 1e-06
LOG2E = 1.4426950408889634
MESH = pl.DeviceIdType.MESH
BF = jnp.bfloat16
F32 = jnp.float32

PIECES = (
    (-1, 0, 0, 48),
    (1, 0, 48, 48),
    (0, -1, 96, 48),
    (0, 1, 144, 48),
    (-1, -1, 192, 16),
    (-1, 1, 208, 16),
    (1, -1, 224, 16),
    (1, 1, 240, 16),
)


def tables():
    span = {-1: range(SIDE - RADIUS, SIDE), 0: range(SIDE), 1: range(RADIUS)}
    pick = np.zeros((COUNT, COUNT), np.float32)
    row = np.full((2 * COUNT,), -100, np.int64)
    col = np.full((2 * COUNT,), -100, np.int64)
    own = np.arange(COUNT)
    row[:COUNT], col[:COUNT] = own // SIDE, own % SIDE
    for side_r, side_c, first, _ in PIECES:
        at = first
        for r in span[side_r]:
            for c in span[side_c]:
                pick[at, r * SIDE + c] = 1
                row[COUNT + at] = r + SIDE * side_r
                col[COUNT + at] = c + SIDE * side_c
                at += 1
    near = (np.abs(row[None] - (own // SIDE)[:, None]) <= RADIUS) & (
        np.abs(col[None] - (own % SIDE)[:, None]) <= RADIUS
    )
    heads = (own[:, None] // HD) == (own[None] // HD)
    table = np.concatenate([pick, near, heads], 1).astype(np.float32)
    place = np.zeros((8, 2 * COUNT), np.int32)
    place[0], place[1] = row, col
    return table, place


def dot(a, b):
    return jnp.dot(a, b, preferred_element_type=F32)


def dot_t(a, b):
    return lax.dot_general(a, b, (((1,), (1,)), ((), ())), preferred_element_type=F32)


def split(values):
    high = values.astype(BF)
    return high, (values - high.astype(F32)).astype(BF)


def rms(values, gain):
    return values * lax.rsqrt(jnp.mean(values * values, -1, keepdims=True) + EPS) * gain


def kernel(
    sizes,
    tokens,
    gain_attn,
    qkv_fine,
    scale_fine,
    out_fine,
    gain_ffn,
    ffn_in,
    ffn_out,
    up_proj,
    gain_coarse,
    qkv_coarse,
    scale_coarse,
    out_coarse,
    table,
    place,
    fine_o,
    coarse_o,
    tok_v,
    ga_v,
    qkv_v,
    out_v,
    gf_v,
    fin_v,
    fout_v,
    up_v,
    gc_v,
    qkvc_v,
    outc_v,
    table_v,
    place_v,
    send_v,
    halo_v,
    fine_v,
    row_v,
    rows_v,
    tile_v,
    tiles_v,
    last_v,
    local_sem,
    halo_send,
    halo_recv,
    row_send,
    row_recv,
    tile_send,
    tile_recv,
):
    n_ha, n_wa = sizes
    n_x, n_z = n_ha // 4, n_wa // 2
    g_row, g_tile = n_z * 2, n_x * 4
    ha, wa = lax.axis_index("ha"), lax.axis_index("wa")
    core = lax.rem(ha, 2)
    x = lax.div(ha, 4)
    z = lax.div(wa, 2)
    y = lax.rem(lax.div(ha, 2), 2) * 2 + lax.rem(wa, 2)

    neighbours = []
    for side_r, side_c, _, _ in PIECES:
        neighbours.append((lax.rem(ha - side_r + n_ha, n_ha), lax.rem(wa - side_c + n_wa, n_wa)))
    row_peers = []
    for d in range(1, g_row):
        to_z = lax.rem(z + d // 2, n_z)
        to_core = lax.rem(core + d % 2, 2)
        row_peers.append((ha - core + to_core, wa - 2 * z + 2 * to_z))
    tile_peers = []
    for d in range(1, g_tile):
        to_x = lax.rem(x + d // 4, n_x)
        to_y = lax.rem(y + d % 4, 4)
        tile_peers.append((4 * to_x + 2 * lax.div(to_y, 2) + core, 2 * z + lax.rem(to_y, 2)))

    barrier = pltpu.get_barrier_semaphore()
    peers = neighbours + row_peers + tile_peers
    for peer in peers:
        pl.semaphore_signal(barrier, inc=1, device_id=peer, device_id_type=MESH)

    loads = {}
    for i, (name, src, dst) in enumerate(
        (
            ("tok", tokens, tok_v),
            ("ga", gain_attn, ga_v),
            ("table", table, table_v),
            ("place", place, place_v),
            ("qkv", qkv_fine, qkv_v),
            ("out", out_fine, out_v),
            ("gf", gain_ffn, gf_v),
            ("fin", ffn_in, fin_v),
            ("fout", ffn_out, fout_v),
            ("up", up_proj, up_v),
            ("gc", gain_coarse, gc_v),
            ("qkvc", qkv_coarse, qkvc_v),
            ("outc", out_coarse, outc_v),
        )
    ):
        loads[name] = pltpu.make_async_copy(src, dst, local_sem.at[i])
        loads[name].start()

    loads["tok"].wait()
    loads["ga"].wait()
    tok = tok_v[...].astype(F32)
    normed = rms(tok, ga_v[...]).astype(BF)
    loads["table"].wait()
    send_v[...] = dot(table_v[:, :COUNT], normed).astype(BF)

    loads["qkv"].wait()
    loads["place"].wait()
    lane_head = lax.broadcasted_iota(jnp.int32, (COUNT, C), 1) // HD
    same = table_v[:, 3 * COUNT : 4 * COUNT]

    def head_scale(values):
        high, low = split(values * values)
        return lax.rsqrt((dot(high, same) + dot(low, same)) * (1 / HD) + EPS)

    def head_norm(values):
        return (values * head_scale(values)).astype(BF)

    pl.semaphore_wait(barrier, len(peers))
    halos = []
    for i, (_, _, first, rows) in enumerate(PIECES):
        copy = pltpu.make_async_remote_copy(
            src_ref=send_v.at[pl.ds(first, rows)],
            dst_ref=halo_v.at[pl.ds(first, rows)],
            send_sem=halo_send.at[i],
            recv_sem=halo_recv.at[i],
            device_id=neighbours[i],
            device_id_type=MESH,
        )
        copy.start()
        halos.append(copy)

    proj = dot(normed, qkv_v[...])
    query = head_norm(proj[:, :C])
    queries = [jnp.where(lane_head == h, query, jnp.zeros_like(query)) for h in range(HEADS)]
    ones = jnp.ones((COUNT, C), BF)
    zero = jnp.zeros((COUNT, C), BF)

    key_row = place_v[0:1, :] + ha * SIDE
    key_col = place_v[1:2, :] + wa * SIDE
    inside = (
        (key_row >= 0) & (key_row < SIDE * n_ha) & (key_col >= 0) & (key_col < SIDE * n_wa)
    ).astype(F32)

    def attend(key, value, part):
        cols = slice(COUNT * (1 + part), COUNT * (2 + part))
        mask = table_v[:, cols].astype(F32) * inside[:, COUNT * part : COUNT * (part + 1)]
        weights, values = [], []
        for h in range(HEADS):
            raw = dot_t(queries[h], key) * (scale_fine[h] * (LOG2E / HD))
            weights.append((jnp.exp2(raw) * mask).astype(BF))
            here = lane_head == h
            values.append(
                jnp.concatenate([jnp.where(here, value, zero), jnp.where(here, ones, zero)], 1)
            )
        return dot(jnp.concatenate(weights, 1), jnp.concatenate(values, 0))

    total = attend(head_norm(proj[:, C : 2 * C]), proj[:, 2 * C :].astype(BF), 0)

    for copy in halos:
        copy.wait_recv()
    proj_h = dot(halo_v[...], qkv_v[:, C:])
    total = total + attend(head_norm(proj_h[:, :C]), proj_h[:, C:].astype(BF), 1)
    attn = (total[:, :C] / total[:, C:]).astype(BF)

    loads["out"].wait()
    loads["gf"].wait()
    h1 = (tok_v[...].astype(F32) + dot(attn, out_v[...])).astype(BF)
    h1f = h1.astype(F32)
    n2 = rms(h1f, gf_v[...]).astype(BF)
    loads["fin"].wait()
    loads["fout"].wait()
    acc = h1f
    for part in range(FFH // C):
        cols = slice(part * C, (part + 1) * C)
        gate = dot(n2, fin_v[:, cols])
        lift = dot(n2, fin_v[:, FFH + part * C : FFH + (part + 1) * C])
        gated = (jax.nn.gelu(gate, approximate=True) * lift).astype(BF)
        acc = acc + dot(gated, fout_v[cols, :])
    fine = acc.astype(BF)
    pooled = jnp.mean(fine.astype(F32), 0, keepdims=True).astype(BF)

    rows_v[0] = pooled.astype(F32)
    row_v[...] = pooled.astype(F32)
    fine_v[...] = fine
    sends = []
    for d, peer in enumerate(row_peers, 1):
        copy = pltpu.make_async_remote_copy(
            src_ref=row_v,
            dst_ref=rows_v.at[d],
            send_sem=row_send.at[d],
            recv_sem=row_recv.at[d],
            device_id=peer,
            device_id_type=MESH,
        )
        copy.start()
        sends.append(copy)
    store = pltpu.make_async_copy(fine_v, fine_o, local_sem.at[13])
    store.start()

    loads["up"].wait()
    loads["gc"].wait()
    loads["qkvc"].wait()
    own = jnp.broadcast_to(pooled.astype(F32), (16, C)).astype(BF)
    coarse_own = dot(own, up_v[...]).astype(BF)
    nc_own = rms(coarse_own.astype(F32), gc_v[...]).astype(BF)
    cq = dot(nc_own, qkvc_v[:, :CC])
    head_of_row = lax.broadcasted_iota(jnp.int32, (HEADS_C, CC), 0)
    head_of_lane = lax.broadcasted_iota(jnp.int32, (HEADS_C, CC), 1) // HD
    diag = head_of_row == head_of_lane
    cq = jnp.where(diag, cq, 0.0)
    cq = cq * lax.rsqrt(jnp.sum(cq * cq, -1, keepdims=True) * (1 / HD) + EPS)
    cq = cq.astype(BF)
    head_sum = jnp.where(diag, 1.0, 0.0).astype(BF)
    scale_col = jnp.zeros((HEADS_C, 1), F32)
    row_id = lax.broadcasted_iota(jnp.int32, (HEADS_C, 1), 0)
    for h in range(HEADS_C):
        scale_col = jnp.where(row_id == h, scale_coarse[h] * (LOG2E / HD), scale_col)

    slot = lax.broadcasted_iota(jnp.int32, (g_row, C), 0)
    tile = jnp.zeros((g_row, C), F32)
    for copy in sends:
        copy.wait_recv()
    for d in range(g_row):
        tile = jnp.where(slot == d, rows_v[d], tile)
    tile_v[...] = tile.astype(BF)
    tiles_v[0] = tile.astype(BF)
    tiles = []
    for d, peer in enumerate(tile_peers, 1):
        copy = pltpu.make_async_remote_copy(
            src_ref=tile_v,
            dst_ref=tiles_v.at[d],
            send_sem=tile_send.at[d],
            recv_sem=tile_recv.at[d],
            device_id=peer,
            device_id_type=MESH,
        )
        copy.start()
        tiles.append(copy)
    for copy in tiles:
        copy.wait_recv()

    every = tiles_v[...].reshape(g_tile * g_row, C)
    coarse = dot(every, up_v[...]).astype(BF)
    nc = rms(coarse.astype(F32), gc_v[...]).astype(BF)
    ck = dot(nc, qkvc_v[:, CC : 2 * CC])
    high, low = split(ck * ck)
    size = (dot_t(head_sum, high) + dot_t(head_sum, low)) * (1 / HD)
    scores = dot_t(cq, ck.astype(BF)) * (lax.rsqrt(size + EPS) * scale_col)
    cexp = jnp.exp2(scores)
    cweights = (cexp / jnp.sum(cexp, -1, keepdims=True)).astype(BF)
    mixed = dot(cweights, nc).astype(BF)
    cattn = jnp.where(diag, dot(mixed, qkvc_v[:, 2 * CC :]), 0.0)
    cattn = jnp.sum(cattn, 0, keepdims=True)
    loads["outc"].wait()
    cattn = jnp.broadcast_to(cattn, (16, CC)).astype(BF)
    result = coarse_own.astype(F32) + dot(cattn, outc_v[...])
    last_v[...] = result[0:1].astype(BF)
    final = pltpu.make_async_copy(last_v, coarse_o, local_sem.at[14])
    final.start()

    for copy in halos + sends + tiles:
        copy.wait_send()
    store.wait()
    final.wait()


def solution(mesh):
    sizes = (mesh.shape["ha"], mesh.shape["wa"])
    g_row, g_tile = sizes[1], sizes[0]
    table, place = tables()
    table, place = jnp.asarray(table, BF), jnp.asarray(place)

    def shards(
        tokens,
        gain_attn,
        qkv_fine,
        scale_fine,
        out_fine,
        gain_ffn,
        ffn_in,
        ffn_out,
        up_proj,
        gain_coarse,
        qkv_coarse,
        scale_coarse,
        out_coarse,
    ):
        hbm = pl.BlockSpec(memory_space=pl.ANY)
        smem = pl.BlockSpec(memory_space=pltpu.SMEM)
        fine, coarse = pl.pallas_call(
            functools.partial(kernel, sizes),
            out_shape=(
                jax.ShapeDtypeStruct((COUNT, C), BF),
                jax.ShapeDtypeStruct((1, CC), BF),
            ),
            in_specs=[hbm, hbm, hbm, smem, hbm, hbm, hbm, hbm, hbm, hbm, hbm, smem, hbm, hbm, hbm],
            out_specs=(hbm, hbm),
            scratch_shapes=[
                pltpu.VMEM((COUNT, C), BF),
                pltpu.VMEM((1, C), F32),
                pltpu.VMEM((C, 3 * C), BF),
                pltpu.VMEM((C, C), BF),
                pltpu.VMEM((1, C), F32),
                pltpu.VMEM((C, 2 * FFH), BF),
                pltpu.VMEM((FFH, C), BF),
                pltpu.VMEM((C, CC), BF),
                pltpu.VMEM((1, CC), F32),
                pltpu.VMEM((CC, 3 * CC), BF),
                pltpu.VMEM((CC, CC), BF),
                pltpu.VMEM((COUNT, 4 * COUNT), BF),
                pltpu.VMEM((8, 2 * COUNT), jnp.int32),
                pltpu.VMEM((COUNT, C), BF),
                pltpu.VMEM((COUNT, C), BF),
                pltpu.VMEM((COUNT, C), BF),
                pltpu.VMEM((1, C), F32),
                pltpu.VMEM((g_row, 1, C), F32),
                pltpu.VMEM((g_row, C), BF),
                pltpu.VMEM((g_tile, g_row, C), BF),
                pltpu.VMEM((1, CC), BF),
                pltpu.SemaphoreType.DMA((15,)),
                pltpu.SemaphoreType.DMA((8,)),
                pltpu.SemaphoreType.DMA((8,)),
                pltpu.SemaphoreType.DMA((g_row,)),
                pltpu.SemaphoreType.DMA((g_row,)),
                pltpu.SemaphoreType.DMA((g_tile,)),
                pltpu.SemaphoreType.DMA((g_tile,)),
            ],
            compiler_params=pltpu.CompilerParams(
                collective_id=0, has_side_effects=True, vmem_limit_bytes=60 * 1024 * 1024
            ),
        )(
            tokens.reshape(COUNT, C),
            gain_attn.reshape(1, C),
            qkv_fine,
            scale_fine,
            out_fine,
            gain_ffn.reshape(1, C),
            ffn_in,
            ffn_out,
            up_proj,
            gain_coarse.reshape(1, CC),
            qkv_coarse,
            scale_coarse,
            out_coarse,
            table,
            place,
        )
        return fine.reshape(SIDE, SIDE, C), coarse.reshape(1, 1, CC)

    return jax.shard_map(
        shards,
        mesh=mesh,
        in_specs=(P("ha", "wa", None),) + (P(),) * 12,
        out_specs=(P("ha", "wa", None), P("ha", "wa", None)),
        check_vma=False,
    )
```

```python
import functools

import jax
import jax.numpy as jnp
import numpy as np
from jax import lax
from jax.experimental import pallas as pl
from jax.experimental.pallas import tpu as pltpu
from jax.sharding import PartitionSpec as P

C = 256
CC = 1024
HD = 64
FFH = 768
RADIUS = 3
SIDE = 16
COUNT = SIDE * SIDE
HEADS = 4
HEADS_C = 16
LANES = 128
EPS = 1e-06
VMEM = 40 * 1024 * 1024
LOG2E = 1.4426950408889634
MESH = pl.DeviceIdType.MESH
BF = jnp.bfloat16
F32 = jnp.float32

PIECES = (
    (-1, 0, 0, 48),
    (1, 0, 48, 48),
    (0, -1, 96, 48),
    (0, 1, 144, 48),
    (-1, -1, 192, 16),
    (-1, 1, 208, 16),
    (1, -1, 224, 16),
    (1, 1, 240, 16),
)


def tables():
    span = {-1: range(SIDE - RADIUS, SIDE), 0: range(SIDE), 1: range(RADIUS)}
    pick = np.zeros((COUNT, COUNT), np.float32)
    row = np.full((2 * COUNT,), -100, np.int64)
    col = np.full((2 * COUNT,), -100, np.int64)
    own = np.arange(COUNT)
    row[:COUNT], col[:COUNT] = own // SIDE, own % SIDE
    for side_r, side_c, first, _ in PIECES:
        at = first
        for r in span[side_r]:
            for c in span[side_c]:
                pick[at, r * SIDE + c] = 1
                row[COUNT + at] = r + SIDE * side_r
                col[COUNT + at] = c + SIDE * side_c
                at += 1
    near = (np.abs(row[None] - (own // SIDE)[:, None]) <= RADIUS) & (
        np.abs(col[None] - (own % SIDE)[:, None]) <= RADIUS
    )
    heads = (own[:, None] // HD) == (own[None] // HD)
    table = np.concatenate([pick, near, heads], 1).astype(np.float32)
    place = np.zeros((8, 2 * COUNT), np.int32)
    place[0], place[1] = row, col
    return table, place


def dot(a, b):
    return jnp.dot(a, b, preferred_element_type=F32)


def dot_t(a, b):
    return lax.dot_general(a, b, (((1,), (1,)), ((), ())), preferred_element_type=F32)


def split(values):
    high = values.astype(BF)
    return high, (values - high.astype(F32)).astype(BF)


def rms(values, gain):
    return values * lax.rsqrt(jnp.mean(values * values, -1, keepdims=True) + EPS) * gain


def kernel(
    sizes,
    tokens,
    gain_attn,
    qkv_fine,
    scale_fine,
    out_fine,
    gain_ffn,
    ffn_in,
    ffn_out,
    up_proj,
    gain_coarse,
    qkv_coarse,
    scale_coarse,
    out_coarse,
    table,
    place,
    fine_o,
    coarse_o,
    tok_v,
    ga_v,
    qkv_v,
    out_v,
    gf_v,
    fin_v,
    fout_v,
    up_v,
    gc_v,
    qkvc_v,
    outc_v,
    table_v,
    place_v,
    sf_s,
    sc_s,
    send_v,
    halo_v,
    row_v,
    rows_v,
    norm_v,
    norms_v,
    tile_v,
    tiles_v,
    ntile_v,
    ntiles_v,
    local_sem,
    halo_send,
    halo_recv,
    row_send,
    row_recv,
    norm_send,
    norm_recv,
    tile_send,
    tile_recv,
    ntile_send,
    ntile_recv,
):
    n_ha, n_wa = sizes
    n_x, n_z = n_ha // 4, n_wa // 2
    g_row, g_tile = n_z * 2, n_x * 4
    ha, wa = lax.axis_index("ha"), lax.axis_index("wa")
    core = lax.rem(ha, 2)
    x = lax.div(ha, 4)
    z = lax.div(wa, 2)
    y = lax.rem(lax.div(ha, 2), 2) * 2 + lax.rem(wa, 2)

    def far(step, count):
        return min(step, count - step)

    neighbours = []
    for side_r, side_c, _, _ in PIECES:
        neighbours.append((lax.rem(ha - side_r + n_ha, n_ha), lax.rem(wa - side_c + n_wa, n_wa)))
    barrier = pltpu.get_barrier_semaphore()
    for peer in neighbours:
        pl.semaphore_signal(barrier, inc=1, device_id=peer, device_id_type=MESH)

    names = ("tok", "ga", "table", "qkv", "place", "sf", "out", "gf", "fin", "fout")
    names += ("up", "gc", "sc", "qkvc", "outc")
    pairs = {
        "tok": (tokens, tok_v),
        "ga": (gain_attn, ga_v),
        "table": (table, table_v),
        "place": (place, place_v),
        "qkv": (qkv_fine, qkv_v),
        "sf": (scale_fine, sf_s),
        "out": (out_fine, out_v),
        "gf": (gain_ffn, gf_v),
        "fin": (ffn_in, fin_v),
        "fout": (ffn_out, fout_v),
        "up": (up_proj, up_v),
        "gc": (gain_coarse, gc_v),
        "sc": (scale_coarse, sc_s),
        "qkvc": (qkv_coarse, qkvc_v),
        "outc": (out_coarse, outc_v),
    }
    loads = {}
    for i, name in enumerate(names):
        loads[name] = pltpu.make_async_copy(*pairs[name], local_sem.at[i])
    for name in names[:6]:
        loads[name].start()

    row_peers = []
    for d in sorted(range(1, g_row), key=lambda d: -far(d // 2, n_z)):
        to_z = lax.rem(z + d // 2, n_z)
        to_core = lax.rem(core + d % 2, 2)
        row_peers.append((d, (ha - core + to_core, wa - 2 * z + 2 * to_z)))
    tile_peers = []
    for d in sorted(range(1, g_tile), key=lambda d: -far(d // 4, n_x) - far(d % 4, 4)):
        to_x = lax.rem(x + d // 4, n_x)
        to_y = lax.rem(y + d % 4, 4)
        peer = (4 * to_x + 2 * lax.div(to_y, 2) + core, 2 * z + lax.rem(to_y, 2))
        tile_peers.append((d, peer))
    for _, peer in row_peers + tile_peers:
        pl.semaphore_signal(barrier, inc=1, device_id=peer, device_id_type=MESH)
    for name in names[6:]:
        loads[name].start()

    def spread(src, dst, send_sem, recv_sem, peers):
        copies = []
        for d, peer in peers:
            copy = pltpu.make_async_remote_copy(
                src_ref=src,
                dst_ref=dst.at[d],
                send_sem=send_sem.at[d],
                recv_sem=recv_sem.at[d],
                device_id=peer,
                device_id_type=MESH,
            )
            copy.start()
            copies.append(copy)
        return copies

    loads["tok"].wait()
    loads["ga"].wait()
    tok = tok_v[...].astype(F32)
    normed = rms(tok, ga_v[...]).astype(BF)
    loads["table"].wait()
    send_v[...] = dot(table_v[:, :COUNT], normed).astype(BF)

    loads["qkv"].wait()
    loads["place"].wait()
    lane_head = lax.broadcasted_iota(jnp.int32, (COUNT, C), 1) // HD
    same = table_v[:, 3 * COUNT : 4 * COUNT]

    def head_scale(values):
        high, low = split(values * values)
        return lax.rsqrt((dot(high, same) + dot(low, same)) * (1 / HD) + EPS)

    def head_norm(values):
        return (values * head_scale(values)).astype(BF)

    pl.semaphore_wait(barrier, len(neighbours) + len(row_peers) + len(tile_peers))
    halos = []
    for i, (_, _, first, rows) in enumerate(PIECES):
        copy = pltpu.make_async_remote_copy(
            src_ref=send_v.at[pl.ds(first, rows)],
            dst_ref=halo_v.at[pl.ds(first, rows)],
            send_sem=halo_send.at[i],
            recv_sem=halo_recv.at[i],
            device_id=neighbours[i],
            device_id_type=MESH,
        )
        copy.start()
        halos.append(copy)

    proj = dot(normed, qkv_v[...])
    query = head_norm(proj[:, :C])
    queries = [jnp.where(lane_head == h, query, jnp.zeros_like(query)) for h in range(HEADS)]
    one, zero = jnp.ones((COUNT, C), BF), jnp.zeros((COUNT, C), BF)

    key_row = place_v[0:1, :] + ha * SIDE
    key_col = place_v[1:2, :] + wa * SIDE
    inside = (
        (key_row >= 0) & (key_row < SIDE * n_ha) & (key_col >= 0) & (key_col < SIDE * n_wa)
    ).astype(F32)

    def attend(key, value, part):
        cols = slice(COUNT * (1 + part), COUNT * (2 + part))
        mask = table_v[:, cols].astype(F32) * inside[:, COUNT * part : COUNT * (part + 1)]
        sums = []
        for first in range(2):
            weights, values = [], []
            for h in range(first, HEADS, 2):
                raw = dot_t(queries[h], key) * (sf_s[h] * (LOG2E / HD))
                weights.append((jnp.exp2(raw) * mask).astype(BF))
                count = jnp.where(lane_head == h + 1 - 2 * first, one, zero)
                values.append(jnp.where(lane_head == h, value, count))
            sums.append(dot(jnp.concatenate(weights, 1), jnp.concatenate(values, 0)))
        return sums

    loads["sf"].wait()
    own_a, own_b = attend(head_norm(proj[:, C : 2 * C]), proj[:, 2 * C :].astype(BF), 0)

    for copy in halos:
        copy.wait_recv()
    proj_h = dot(halo_v[...], qkv_v[:, C:])
    halo_a, halo_b = attend(head_norm(proj_h[:, :C]), proj_h[:, C:].astype(BF), 1)
    sum_a, sum_b = own_a + halo_a, own_b + halo_b
    even = lax.rem(lane_head, 2) == 0
    over = jnp.where(even, sum_a, sum_b)
    under = jnp.where(even, sum_b, sum_a)
    under = jnp.concatenate(
        [pltpu.roll(under[:, :128], HD, 1), pltpu.roll(under[:, 128:], HD, 1)], 1
    )
    attn = (over / under).astype(BF)

    loads["out"].wait()
    loads["gf"].wait()
    h1 = (tok_v[...].astype(F32) + dot(attn, out_v[...])).astype(BF)
    h1f = h1.astype(F32)
    n2 = rms(h1f, gf_v[...]).astype(BF)
    loads["fin"].wait()
    loads["fout"].wait()
    acc = h1f
    for part in range(FFH // C):
        cols = slice(part * C, (part + 1) * C)
        gate = dot(n2, fin_v[:, cols])
        lift = dot(n2, fin_v[:, FFH + part * C : FFH + (part + 1) * C])
        gated = (jax.nn.gelu(gate, approximate=True) * lift).astype(BF)
        acc = acc + dot(gated, fout_v[cols, :])
    fine = acc.astype(BF)
    pooled = jnp.mean(fine.astype(F32), 0, keepdims=True).astype(BF)

    row = pooled.astype(F32)
    row_v[...] = row
    rows = spread(row_v, rows_v, row_send, row_recv, row_peers)
    fine_o[...] = fine

    loads["up"].wait()
    loads["gc"].wait()
    loads["sc"].wait()
    loads["qkvc"].wait()
    own = jnp.broadcast_to(row, (HEADS_C, C)).astype(BF)
    coarse_own = dot(own, up_v[...]).astype(BF)
    coarse_f = coarse_own.astype(F32)
    factor = lax.rsqrt(jnp.mean(coarse_f * coarse_f, -1, keepdims=True) + EPS)
    nc_own = (coarse_f * factor * gc_v[...]).astype(BF)
    cqk = dot(nc_own, qkvc_v[:, : 2 * CC])
    head_of_row = lax.broadcasted_iota(jnp.int32, (HEADS_C, CC), 0)
    diag = head_of_row == lax.broadcasted_iota(jnp.int32, (HEADS_C, CC), 1) // HD

    def norm_of(values):
        return lax.rsqrt(jnp.sum(values * values, -1, keepdims=True) * (1 / HD) + EPS)

    ck = jnp.where(diag, cqk[:, CC:], 0.0)
    slot = lax.broadcasted_iota(jnp.int32, (HEADS_C, LANES), 0)
    lane = lax.broadcasted_iota(jnp.int32, (HEADS_C, LANES), 1)
    scales = jnp.zeros((HEADS_C, 1), F32)
    for h in range(HEADS_C):
        scales = jnp.where(slot[:, 0:1] == h, sc_s[h] * (LOG2E / HD), scales)
    norms = jnp.where(slot == lane, norm_of(ck) * factor * scales, 0.0)
    norms = jnp.sum(norms, 0, keepdims=True)
    norms = jnp.where(lane[0:1] == HEADS_C, factor[0:1], norms)
    norm_v[...] = norms
    more = spread(norm_v, norms_v, norm_send, norm_recv, row_peers)
    cq = jnp.where(diag, cqk[:, :CC], 0.0)
    cq = (cq * norm_of(cq)).astype(BF)

    def gathered(own_row, others, width):
        at = lax.broadcasted_iota(jnp.int32, (g_row, width), 0)
        tile = jnp.broadcast_to(own_row, (g_row, width))
        for d in range(1, g_row):
            tile = jnp.where(at == d, others[d], tile)
        return tile

    for copy in rows:
        copy.wait_recv()
    tile = gathered(row, rows_v, C).astype(BF)
    tile_v[...] = tile
    tiles = spread(tile_v, tiles_v, tile_send, tile_recv, tile_peers)
    tiles_v[0] = tile
    for copy in more:
        copy.wait_recv()
    tile = gathered(norms, norms_v, LANES)
    ntile_v[...] = tile
    ntiles = spread(ntile_v, ntiles_v, ntile_send, ntile_recv, tile_peers)
    ntiles_v[0] = tile

    back = dot_t(cq, qkvc_v[:, CC : 2 * CC]) * gc_v[...]
    back = dot_t(jnp.concatenate(split(back), 0), up_v[...])
    back = jnp.concatenate(split(back[:HEADS_C] + back[HEADS_C:]), 1)

    for copy in tiles:
        copy.wait_recv()
    every = tiles_v[...].reshape(g_tile * g_row, C)
    scores = dot_t(back, jnp.concatenate([every, every], 1))
    for copy in ntiles:
        copy.wait_recv()
    norms = ntiles_v[...].reshape(g_tile * g_row, LANES).T
    cexp = jnp.exp2(scores * norms[:HEADS_C])
    cweights = (cexp / jnp.sum(cexp, -1, keepdims=True)) * norms[HEADS_C : HEADS_C + 1]
    mixed = dot(jnp.concatenate(split(cweights), 0), every)
    mixed = mixed[:HEADS_C] + mixed[HEADS_C:]
    mixed = dot(jnp.concatenate(split(mixed), 0), up_v[...])
    mixed = ((mixed[:HEADS_C] + mixed[HEADS_C:]) * gc_v[...]).astype(BF)
    cattn = jnp.where(diag, dot(mixed, qkvc_v[:, 2 * CC :]), 0.0)
    cattn = jnp.sum(cattn, 0, keepdims=True)
    loads["outc"].wait()
    cattn = jnp.broadcast_to(cattn, (HEADS_C, CC)).astype(BF)
    result = coarse_f + dot(cattn, outc_v[...])
    coarse_o[...] = result[0:1].astype(BF)

    for copy in halos + rows + more + tiles + ntiles:
        copy.wait_send()


def finish(fine, coarse, fine_o, coarse_o, sem):
    copies = [
        pltpu.make_async_copy(fine, fine_o, sem.at[0]),
        pltpu.make_async_copy(coarse, coarse_o, sem.at[1]),
    ]
    for copy in copies:
        copy.start()
    for copy in copies:
        copy.wait()


def solution(mesh):
    sizes = (mesh.shape["ha"], mesh.shape["wa"])
    g_row, g_tile = sizes[1], sizes[0]
    table, place = tables()
    table, place = jnp.asarray(table, BF), jnp.asarray(place)

    def shards(
        tokens,
        gain_attn,
        qkv_fine,
        scale_fine,
        out_fine,
        gain_ffn,
        ffn_in,
        ffn_out,
        up_proj,
        gain_coarse,
        qkv_coarse,
        scale_coarse,
        out_coarse,
    ):
        hbm = pl.BlockSpec(memory_space=pl.ANY)
        fine, coarse = pl.pallas_call(
            functools.partial(kernel, sizes),
            out_shape=(pltpu.VMEM((COUNT, C), BF), pltpu.VMEM((1, CC), BF)),
            in_specs=[hbm] * 15,
            out_specs=(pl.BlockSpec(memory_space=pltpu.VMEM),) * 2,
            scratch_shapes=[
                pltpu.VMEM((COUNT, C), BF),
                pltpu.VMEM((1, C), F32),
                pltpu.VMEM((C, 3 * C), BF),
                pltpu.VMEM((C, C), BF),
                pltpu.VMEM((1, C), F32),
                pltpu.VMEM((C, 2 * FFH), BF),
                pltpu.VMEM((FFH, C), BF),
                pltpu.VMEM((C, CC), BF),
                pltpu.VMEM((1, CC), F32),
                pltpu.VMEM((CC, 3 * CC), BF),
                pltpu.VMEM((CC, CC), BF),
                pltpu.VMEM((COUNT, 4 * COUNT), BF),
                pltpu.VMEM((8, 2 * COUNT), jnp.int32),
                pltpu.SMEM((HEADS,), F32),
                pltpu.SMEM((HEADS_C,), F32),
                pltpu.VMEM((COUNT, C), BF),
                pltpu.VMEM((COUNT, C), BF),
                pltpu.VMEM((1, C), F32),
                pltpu.VMEM((g_row, 1, C), F32),
                pltpu.VMEM((1, LANES), F32),
                pltpu.VMEM((g_row, 1, LANES), F32),
                pltpu.VMEM((g_row, C), BF),
                pltpu.VMEM((g_tile, g_row, C), BF),
                pltpu.VMEM((g_row, LANES), F32),
                pltpu.VMEM((g_tile, g_row, LANES), F32),
                pltpu.SemaphoreType.DMA((15,)),
                pltpu.SemaphoreType.DMA((8,)),
                pltpu.SemaphoreType.DMA((8,)),
                pltpu.SemaphoreType.DMA((g_row,)),
                pltpu.SemaphoreType.DMA((g_row,)),
                pltpu.SemaphoreType.DMA((g_row,)),
                pltpu.SemaphoreType.DMA((g_row,)),
                pltpu.SemaphoreType.DMA((g_tile,)),
                pltpu.SemaphoreType.DMA((g_tile,)),
                pltpu.SemaphoreType.DMA((g_tile,)),
                pltpu.SemaphoreType.DMA((g_tile,)),
            ],
            compiler_params=pltpu.CompilerParams(
                collective_id=0, has_side_effects=True, vmem_limit_bytes=VMEM
            ),
        )(*[pltpu.with_memory_space_constraint(v, pltpu.HBM) for v in (
            tokens.reshape(COUNT, C),
            gain_attn.reshape(1, C),
            qkv_fine,
            scale_fine,
            out_fine,
            gain_ffn.reshape(1, C),
            ffn_in,
            ffn_out,
            up_proj,
            gain_coarse.reshape(1, CC),
            qkv_coarse,
            scale_coarse,
            out_coarse,
            table,
            place,
        )])
        fine, coarse = pl.pallas_call(
            finish,
            out_shape=(
                jax.ShapeDtypeStruct((COUNT, C), BF),
                jax.ShapeDtypeStruct((1, CC), BF),
            ),
            in_specs=[pl.BlockSpec(memory_space=pltpu.VMEM)] * 2,
            out_specs=(pl.BlockSpec(memory_space=pltpu.HBM),) * 2,
            scratch_shapes=[pltpu.SemaphoreType.DMA((2,))],
            compiler_params=pltpu.CompilerParams(vmem_limit_bytes=1024 * 1024),
        )(fine, coarse)
        return fine.reshape(SIDE, SIDE, C), coarse.reshape(1, 1, CC)

    return jax.shard_map(
        shards,
        mesh=mesh,
        in_specs=(P("ha", "wa", None),) + (P(),) * 12,
        out_specs=(P("ha", "wa", None), P("ha", "wa", None)),
        check_vma=False,
    )
```

```python
import functools

import jax
import jax.numpy as jnp
import numpy as np
from jax import lax
from jax.experimental import pallas as pl
from jax.experimental.pallas import tpu as pltpu
from jax.sharding import PartitionSpec as P

C = 256
CC = 1024
HD = 64
FFH = 768
RADIUS = 3
SIDE = 16
COUNT = SIDE * SIDE
EDGE = 160
HEADS = 4
HEADS_C = 16
LANES = 128
EPS = 1e-06
VMEM = 40 * 1024 * 1024
LOG2E = 1.4426950408889634
GELU = 0.7978845608028654
MESH = pl.DeviceIdType.MESH
BF = jnp.bfloat16
F32 = jnp.float32

PIECES = (
    (-1, 0, 0, 48),
    (1, 0, 48, 48),
    (0, -1, 96, 48),
    (0, 1, 144, 48),
    (-1, -1, 192, 16),
    (-1, 1, 208, 16),
    (1, -1, 224, 16),
    (1, 1, 240, 16),
)


def tables():
    span = {-1: range(SIDE - RADIUS, SIDE), 0: range(SIDE), 1: range(RADIUS)}
    pick = np.zeros((COUNT, COUNT))
    row = np.full((COUNT,), -100, np.int32)
    col = np.full((COUNT,), -100, np.int32)
    for side_r, side_c, first, _ in PIECES:
        at = first
        for r in span[side_r]:
            for c in span[side_c]:
                pick[at, r * SIDE + c] = 1
                row[at] = r + SIDE * side_r
                col[at] = c + SIDE * side_c
                at += 1
    natural = np.arange(COUNT)
    own_r, own_c = natural // SIDE, natural % SIDE
    inner = np.minimum(
        np.minimum(own_r, SIDE - 1 - own_r), np.minimum(own_c, SIDE - 1 - own_c)
    )
    order = np.argsort(inner, kind="stable")
    perm = np.eye(COUNT)[order]
    own_r, own_c = own_r[order][:, None], own_c[order][:, None]

    def near(key_r, key_c):
        return (np.abs(key_r - own_r) <= RADIUS) & (np.abs(key_c - own_c) <= RADIUS)

    heads = (natural[:, None] // HD) == (natural[None] // HD)
    parts = [perm, perm.T, near(natural // SIDE, natural % SIDE), near(row[None], col[None])]
    place = np.zeros((8, COUNT), np.int32)
    place[0], place[1] = row, col
    return np.concatenate([pick, heads], 1), np.concatenate(parts, 1), place


def dot(a, b):
    return jnp.dot(a, b, preferred_element_type=F32)


def dot_t(a, b):
    return lax.dot_general(a, b, (((1,), (1,)), ((), ())), preferred_element_type=F32)


def split(values):
    high = values.astype(BF)
    return high, (values - high.astype(F32)).astype(BF)


def rms(values, gain):
    return values * lax.rsqrt(jnp.mean(values * values, -1, keepdims=True) + EPS) * gain


def kernel(
    sizes,
    tokens,
    gain_attn,
    qkv_fine,
    scale_fine,
    out_fine,
    gain_ffn,
    ffn_in,
    ffn_out,
    up_proj,
    gain_coarse,
    qkv_coarse,
    scale_coarse,
    out_coarse,
    pick,
    table,
    place,
    fine_o,
    coarse_o,
    tok_v,
    ga_v,
    qkv_v,
    out_v,
    gf_v,
    fin_v,
    fout_v,
    up_v,
    gc_v,
    qkvc_v,
    outc_v,
    pick_v,
    table_v,
    place_v,
    sf_s,
    sc_s,
    send_v,
    halo_v,
    tok_p,
    own_v,
    mask_v,
    part_v,
    fine_v,
    out_m,
    row_v,
    rows_v,
    norm_v,
    norms_v,
    tile_v,
    tiles_v,
    ntile_v,
    ntiles_v,
    local_sem,
    halo_send,
    halo_recv,
    row_send,
    row_recv,
    norm_send,
    norm_recv,
    tile_send,
    tile_recv,
    ntile_send,
    ntile_recv,
):
    n_ha, n_wa = sizes
    n_x, n_z = n_ha // 4, n_wa // 2
    g_row, g_tile = n_z * 2, n_x * 4
    ha, wa = lax.axis_index("ha"), lax.axis_index("wa")
    core = lax.rem(ha, 2)
    x = lax.div(ha, 4)
    z = lax.div(wa, 2)
    y = lax.rem(lax.div(ha, 2), 2) * 2 + lax.rem(wa, 2)

    def far(step, count):
        return min(step, count - step)

    neighbours = []
    for side_r, side_c, _, _ in PIECES:
        neighbours.append((lax.rem(ha - side_r + n_ha, n_ha), lax.rem(wa - side_c + n_wa, n_wa)))
    row_peers = []
    for d in sorted(range(1, g_row), key=lambda d: -far(d // 2, n_z)):
        to_z = lax.rem(z + d // 2, n_z)
        to_core = lax.rem(core + d % 2, 2)
        row_peers.append((d, (ha - core + to_core, wa - 2 * z + 2 * to_z)))
    tile_peers = []
    for d in sorted(range(1, g_tile), key=lambda d: -far(d // 4, n_x) - far(d % 4, 4)):
        to_x = lax.rem(x + d // 4, n_x)
        to_y = lax.rem(y + d % 4, 4)
        peer = (4 * to_x + 2 * lax.div(to_y, 2) + core, 2 * z + lax.rem(to_y, 2))
        tile_peers.append((d, peer))
    names = ("tok", "ga", "qkv", "pick", "table", "place", "sf", "out", "gf", "fin", "fout")
    names += ("up", "gc", "sc", "qkvc", "outc")
    pairs = {
        "tok": (tokens, tok_v),
        "ga": (gain_attn, ga_v),
        "pick": (pick, pick_v),
        "table": (table, table_v),
        "place": (place, place_v),
        "qkv": (qkv_fine, qkv_v),
        "sf": (scale_fine, sf_s),
        "out": (out_fine, out_v),
        "gf": (gain_ffn, gf_v),
        "fin": (ffn_in, fin_v),
        "fout": (ffn_out, fout_v),
        "up": (up_proj, up_v),
        "gc": (gain_coarse, gc_v),
        "sc": (scale_coarse, sc_s),
        "qkvc": (qkv_coarse, qkvc_v),
        "outc": (out_coarse, outc_v),
    }
    loads = {}
    for i, name in enumerate(names):
        loads[name] = pltpu.make_async_copy(*pairs[name], local_sem.at[i])
    for name in names[:4]:
        loads[name].start()
    barrier = pltpu.get_barrier_semaphore()
    hops = [(far(d // 2, n_z), peer) for d, peer in row_peers]
    hops += [(far(d // 4, n_x) + far(d % 4, 4), peer) for d, peer in tile_peers]
    hops += [(3 if PIECES[i][0] else 2, peer) for i, peer in enumerate(neighbours)]
    for _, peer in sorted(hops, key=lambda hop: -hop[0]):
        pl.semaphore_signal(barrier, inc=1, device_id=peer, device_id_type=MESH)

    for name in names[4:]:
        loads[name].start()

    def spread(src, dst, send_sem, recv_sem, peers):
        for d, peer in peers:
            pltpu.make_async_remote_copy(
                src_ref=src,
                dst_ref=dst.at[d],
                send_sem=send_sem,
                recv_sem=recv_sem,
                device_id=peer,
                device_id_type=MESH,
            ).start()
        others = dst.at[pl.ds(1, len(peers))]
        return pltpu.make_async_remote_copy(
            src_ref=others,
            dst_ref=others,
            send_sem=send_sem,
            recv_sem=recv_sem,
            device_id=peers[0][1],
            device_id_type=MESH,
        )

    loads["tok"].wait()
    loads["ga"].wait()
    normed = rms(tok_v[...].astype(F32), ga_v[...]).astype(BF)
    loads["qkv"].wait()
    proj = dot(normed, qkv_v[...])
    loads["pick"].wait()
    same = pick_v[:, COUNT:]

    def head_norm(values):
        high, low = split(values * values)
        size = (dot(high, same) + dot(low, same)) * (1 / HD)
        return values * lax.rsqrt(size + EPS)

    key, value = head_norm(proj[:, C : 2 * C]).astype(BF), proj[:, 2 * C :].astype(BF)
    send_v[...] = dot(pick_v[:, :COUNT], jnp.concatenate([key, value], 1)).astype(BF)

    pl.semaphore_wait(barrier, len(neighbours) + len(row_peers) + len(tile_peers))
    for i, (_, _, first, rows) in enumerate(PIECES):
        pltpu.make_async_remote_copy(
            src_ref=send_v.at[pl.ds(first, rows)],
            dst_ref=halo_v.at[pl.ds(first, rows)],
            send_sem=halo_send,
            recv_sem=halo_recv,
            device_id=neighbours[i],
            device_id_type=MESH,
        ).start()
    halos = pltpu.make_async_remote_copy(
        src_ref=send_v,
        dst_ref=halo_v,
        send_sem=halo_send,
        recv_sem=halo_recv,
        device_id=neighbours[0],
        device_id_type=MESH,
    )

    loads["table"].wait()
    loads["place"].wait()
    loads["sf"].wait()
    perm = table_v[:, :COUNT]
    tok_p[...] = dot(perm, tok_v[...]).astype(BF)
    lane_head = lax.broadcasted_iota(jnp.int32, (COUNT, C), 1) // HD
    scales = jnp.zeros((1, C), F32)
    for h in range(HEADS):
        scales = jnp.where(lane_head[0:1] == h, sf_s[h] * (LOG2E / HD), scales)
    query = dot(perm, (head_norm(proj[:, :C]) * scales).astype(BF)).astype(BF)
    zero, one = jnp.zeros((COUNT, C), BF), jnp.ones((COUNT, C), BF)
    queries = [jnp.where(lane_head == h, query, zero) for h in range(HEADS)]

    key_row = place_v[0:1, :] + ha * SIDE
    key_col = place_v[1:2, :] + wa * SIDE
    inside = (
        (key_row >= 0) & (key_row < SIDE * n_ha) & (key_col >= 0) & (key_col < SIDE * n_wa)
    ).astype(F32)
    mask_v[...] = table_v[:EDGE, 3 * COUNT : 4 * COUNT].astype(F32) * inside

    def attend(rows, keys, value, mask):
        sums = []
        for first in range(2):
            weights, values = [], []
            for h in range(first, HEADS, 2):
                raw = dot_t(queries[h][:rows], keys)
                weights.append((jnp.exp2(raw) * mask).astype(BF))
                count = jnp.where(lane_head == h + 1 - 2 * first, one, zero)
                values.append(jnp.where(lane_head == h, value, count))
            sums.append(dot(jnp.concatenate(weights, 1), jnp.concatenate(values, 0)))
        return sums

    def finished(sum_a, sum_b, tok):
        even = lax.rem(lane_head[: tok.shape[0]], 2) == 0
        over = jnp.where(even, sum_a, sum_b)
        under = jnp.where(even, sum_b, sum_a)
        under = jnp.concatenate(
            [pltpu.roll(under[:, :LANES], HD, 1), pltpu.roll(under[:, LANES:], HD, 1)], 1
        )
        attn = (over / under).astype(BF)
        h1 = (tok.astype(F32) + dot(attn, out_v[...])).astype(BF)
        h1 = h1.astype(F32)
        n2 = rms(h1, gf_v[...]).astype(BF)
        acc = 0.0
        for part in range(FFH // C):
            gate = dot(n2, fin_v[:, part * C : (part + 1) * C])
            lift = dot(n2, fin_v[:, FFH + part * C : FFH + (part + 1) * C])
            bend = jnp.tanh(gate * (GELU + (GELU * 0.044715) * (gate * gate)))
            gated = (gate * lift * (1.0 + bend)).astype(BF)
            acc = acc + dot(gated, fout_v[part * C : (part + 1) * C, :])
        return (h1 + 0.5 * acc).astype(BF)

    own_mask = table_v[:, 2 * COUNT : 3 * COUNT].astype(F32)
    sum_a, sum_b = attend(COUNT, key, value, own_mask)
    own_v[0] = sum_a[:EDGE]
    own_v[1] = sum_b[:EDGE]
    for name in ("out", "gf", "fin", "fout"):
        loads[name].wait()
    fine = finished(sum_a[EDGE:], sum_b[EDGE:], tok_p[EDGE:, :])
    fine_v[EDGE:, :] = fine
    part_v[...] = jnp.sum(fine.astype(F32), 0, keepdims=True)

    halos.wait_recv()
    sum_a, sum_b = attend(EDGE, halo_v[:, :C], halo_v[:, C:], mask_v[...])
    fine = finished(own_v[0] + sum_a, own_v[1] + sum_b, tok_p[:EDGE, :])
    fine_v[:EDGE, :] = fine
    pooled = part_v[...] + jnp.sum(fine.astype(F32), 0, keepdims=True)
    pooled = (pooled * (1 / COUNT)).astype(BF)

    row = pooled.astype(F32)
    row_v[...] = row
    rows = spread(row_v, rows_v, row_send, row_recv, row_peers)
    fine_o[...] = dot(table_v[:, COUNT : 2 * COUNT], fine_v[...]).astype(BF)

    loads["up"].wait()
    loads["gc"].wait()
    loads["sc"].wait()
    loads["qkvc"].wait()
    own = jnp.broadcast_to(row, (HEADS_C, C)).astype(BF)
    coarse_own = dot(own, up_v[...]).astype(BF)
    coarse_f = coarse_own.astype(F32)
    factor = lax.rsqrt(jnp.mean(coarse_f * coarse_f, -1, keepdims=True) + EPS)
    nc_own = (coarse_f * factor * gc_v[...]).astype(BF)
    cqk = dot(nc_own, qkvc_v[:, : 2 * CC])
    head_of_row = lax.broadcasted_iota(jnp.int32, (HEADS_C, CC), 0)
    diag = head_of_row == lax.broadcasted_iota(jnp.int32, (HEADS_C, CC), 1) // HD

    def norm_of(values):
        return lax.rsqrt(jnp.sum(values * values, -1, keepdims=True) * (1 / HD) + EPS)

    ck = jnp.where(diag, cqk[:, CC:], 0.0)
    slot = lax.broadcasted_iota(jnp.int32, (HEADS_C, LANES), 0)
    lane = lax.broadcasted_iota(jnp.int32, (HEADS_C, LANES), 1)
    scales = jnp.zeros((HEADS_C, 1), F32)
    for h in range(HEADS_C):
        scales = jnp.where(slot[:, 0:1] == h, sc_s[h] * (LOG2E / HD), scales)
    norms = jnp.where(slot == lane, norm_of(ck) * factor * scales, 0.0)
    norms = jnp.sum(norms, 0, keepdims=True)
    norms = jnp.where(lane[0:1] == HEADS_C, factor[0:1], norms)
    norm_v[...] = norms
    more = spread(norm_v, norms_v, norm_send, norm_recv, row_peers)
    cq = jnp.where(diag, cqk[:, :CC], 0.0)
    cq = (cq * norm_of(cq)).astype(BF)

    back = dot_t(cq, qkvc_v[:, CC : 2 * CC]) * gc_v[...]
    back = dot_t(jnp.concatenate(split(back), 0), up_v[...])
    back = jnp.concatenate(split(back[:HEADS_C] + back[HEADS_C:]), 1)

    def gathered(own_row, others, width):
        at = lax.broadcasted_iota(jnp.int32, (g_row, width), 0)
        tile = jnp.broadcast_to(own_row, (g_row, width))
        for d in range(1, g_row):
            tile = jnp.where(at == d, others[d], tile)
        return tile

    rows.wait_recv()
    tile = gathered(row, rows_v, C).astype(BF)
    tile_v[...] = tile
    tiles = spread(tile_v, tiles_v, tile_send, tile_recv, tile_peers)
    tiles_v[0] = tile
    more.wait_recv()
    tile = gathered(norms, norms_v, LANES)
    ntile_v[...] = tile
    ntiles = spread(ntile_v, ntiles_v, ntile_send, ntile_recv, tile_peers)
    ntiles_v[0] = tile

    high, low = split(up_v[...].astype(F32) * gc_v[...])
    value = qkvc_v[:, 2 * CC :]
    out_m[...] = (dot(high, value) + dot(low, value)).astype(BF)

    tiles.wait_recv()
    every = tiles_v[...].reshape(g_tile * g_row, C)
    scores = dot_t(back, jnp.concatenate([every, every], 1))
    ntiles.wait_recv()
    norms = ntiles_v[...].reshape(g_tile * g_row, LANES).T
    cexp = jnp.exp2(scores * norms[:HEADS_C])
    cweights = (cexp / jnp.sum(cexp, -1, keepdims=True)) * norms[HEADS_C : HEADS_C + 1]
    mixed = dot(jnp.concatenate(split(cweights), 0), every)
    mixed = mixed[:HEADS_C] + mixed[HEADS_C:]
    mixed = dot(jnp.concatenate(split(mixed), 0), out_m[...])
    cattn = jnp.where(diag, mixed[:HEADS_C] + mixed[HEADS_C:], 0.0)
    cattn = jnp.sum(cattn, 0, keepdims=True)
    loads["outc"].wait()
    cattn = jnp.broadcast_to(cattn, (HEADS_C, CC)).astype(BF)
    result = coarse_f + dot(cattn, outc_v[...])
    coarse_o[...] = result[0:1].astype(BF)

    for copy in (halos, rows, more, tiles, ntiles):
        copy.wait_send()


def finish(fine, coarse, fine_o, coarse_o, sem):
    copies = [
        pltpu.make_async_copy(fine, fine_o, sem.at[0]),
        pltpu.make_async_copy(coarse, coarse_o, sem.at[1]),
    ]
    for copy in copies:
        copy.start()
    for copy in copies:
        copy.wait()


def solution(mesh):
    sizes = (mesh.shape["ha"], mesh.shape["wa"])
    g_row, g_tile = sizes[1], sizes[0]
    pick, table, place = tables()
    pick, table = jnp.asarray(pick, BF), jnp.asarray(table, BF)
    place = jnp.asarray(place)

    def shards(
        tokens,
        gain_attn,
        qkv_fine,
        scale_fine,
        out_fine,
        gain_ffn,
        ffn_in,
        ffn_out,
        up_proj,
        gain_coarse,
        qkv_coarse,
        scale_coarse,
        out_coarse,
    ):
        hbm = pl.BlockSpec(memory_space=pl.ANY)
        fine, coarse = pl.pallas_call(
            functools.partial(kernel, sizes),
            out_shape=(pltpu.VMEM((COUNT, C), BF), pltpu.VMEM((1, CC), BF)),
            in_specs=[hbm] * 16,
            out_specs=(pl.BlockSpec(memory_space=pltpu.VMEM),) * 2,
            scratch_shapes=[
                pltpu.VMEM((COUNT, C), BF),
                pltpu.VMEM((1, C), F32),
                pltpu.VMEM((C, 3 * C), BF),
                pltpu.VMEM((C, C), BF),
                pltpu.VMEM((1, C), F32),
                pltpu.VMEM((C, 2 * FFH), BF),
                pltpu.VMEM((FFH, C), BF),
                pltpu.VMEM((C, CC), BF),
                pltpu.VMEM((1, CC), F32),
                pltpu.VMEM((CC, 3 * CC), BF),
                pltpu.VMEM((CC, CC), BF),
                pltpu.VMEM((COUNT, 2 * COUNT), BF),
                pltpu.VMEM((COUNT, 4 * COUNT), BF),
                pltpu.VMEM((8, COUNT), jnp.int32),
                pltpu.SMEM((HEADS,), F32),
                pltpu.SMEM((HEADS_C,), F32),
                pltpu.VMEM((COUNT, 2 * C), BF),
                pltpu.VMEM((COUNT, 2 * C), BF),
                pltpu.VMEM((COUNT, C), BF),
                pltpu.VMEM((2, EDGE, C), F32),
                pltpu.VMEM((EDGE, COUNT), F32),
                pltpu.VMEM((1, C), F32),
                pltpu.VMEM((COUNT, C), BF),
                pltpu.VMEM((C, CC), BF),
                pltpu.VMEM((1, C), F32),
                pltpu.VMEM((g_row, 1, C), F32),
                pltpu.VMEM((1, LANES), F32),
                pltpu.VMEM((g_row, 1, LANES), F32),
                pltpu.VMEM((g_row, C), BF),
                pltpu.VMEM((g_tile, g_row, C), BF),
                pltpu.VMEM((g_row, LANES), F32),
                pltpu.VMEM((g_tile, g_row, LANES), F32),
                pltpu.SemaphoreType.DMA((16,)),
                *[pltpu.SemaphoreType.DMA] * 10,
            ],
            compiler_params=pltpu.CompilerParams(
                collective_id=0, has_side_effects=True, vmem_limit_bytes=VMEM
            ),
        )(*[pltpu.with_memory_space_constraint(v, pltpu.HBM) for v in (
            tokens.reshape(COUNT, C),
            gain_attn.reshape(1, C),
            qkv_fine,
            scale_fine,
            out_fine,
            gain_ffn.reshape(1, C),
            ffn_in,
            ffn_out,
            up_proj,
            gain_coarse.reshape(1, CC),
            qkv_coarse,
            scale_coarse,
            out_coarse,
            pick,
            table,
            place,
        )])
        fine, coarse = pl.pallas_call(
            finish,
            out_shape=(
                jax.ShapeDtypeStruct((COUNT, C), BF),
                jax.ShapeDtypeStruct((1, CC), BF),
            ),
            in_specs=[pl.BlockSpec(memory_space=pltpu.VMEM)] * 2,
            out_specs=(pl.BlockSpec(memory_space=pltpu.HBM),) * 2,
            scratch_shapes=[pltpu.SemaphoreType.DMA((2,))],
            compiler_params=pltpu.CompilerParams(vmem_limit_bytes=1024 * 1024),
        )(fine, coarse)
        return fine.reshape(SIDE, SIDE, C), coarse.reshape(1, 1, CC)

    return jax.shard_map(
        shards,
        mesh=mesh,
        in_specs=(P("ha", "wa", None),) + (P(),) * 12,
        out_specs=(P("ha", "wa", None), P("ha", "wa", None)),
        check_vma=False,
    )
```

```python
import functools

import jax
import jax.numpy as jnp
import numpy as np
from jax import lax
from jax.experimental import pallas as pl
from jax.experimental.pallas import tpu as pltpu
from jax.sharding import PartitionSpec as P

C = 256
CC = 1024
HD = 64
FFH = 768
RADIUS = 3
SIDE = 16
COUNT = SIDE * SIDE
EDGE = 160
HEADS = 4
HEADS_C = 16
LANES = 128
EPS = 1e-06
VMEM = 40 * 1024 * 1024
LOG2E = 1.4426950408889634
GELU = 0.7978845608028654
MESH = pl.DeviceIdType.MESH
BF = jnp.bfloat16
F32 = jnp.float32

PIECES = (
    (-1, 0, 0, 48),
    (1, 0, 48, 48),
    (0, -1, 96, 48),
    (0, 1, 144, 48),
    (-1, -1, 192, 16),
    (-1, 1, 208, 16),
    (1, -1, 224, 16),
    (1, 1, 240, 16),
)


def tables():
    span = {-1: range(SIDE - RADIUS, SIDE), 0: range(SIDE), 1: range(RADIUS)}
    pick = np.zeros((COUNT, COUNT))
    row = np.full((COUNT,), -100, np.int32)
    col = np.full((COUNT,), -100, np.int32)
    for side_r, side_c, first, _ in PIECES:
        at = first
        for r in span[side_r]:
            for c in span[side_c]:
                pick[at, r * SIDE + c] = 1
                row[at] = r + SIDE * side_r
                col[at] = c + SIDE * side_c
                at += 1
    natural = np.arange(COUNT)
    own_r, own_c = natural // SIDE, natural % SIDE
    inner = np.minimum(
        np.minimum(own_r, SIDE - 1 - own_r), np.minimum(own_c, SIDE - 1 - own_c)
    )
    order = np.argsort(inner, kind="stable")
    perm = np.eye(COUNT)[order]
    own_r, own_c = own_r[order][:, None], own_c[order][:, None]

    def near(key_r, key_c):
        return (np.abs(key_r - own_r) <= RADIUS) & (np.abs(key_c - own_c) <= RADIUS)

    heads = (natural[:, None] // HD) == (natural[None] // HD)
    parts = [perm, perm.T, near(natural // SIDE, natural % SIDE), near(row[None], col[None])]
    place = np.zeros((8, COUNT), np.int32)
    place[0], place[1] = row, col
    return np.concatenate([pick, heads], 1), np.concatenate(parts, 1), place


def dot(a, b):
    return jnp.dot(a, b, preferred_element_type=F32)


def dot_t(a, b):
    return lax.dot_general(a, b, (((1,), (1,)), ((), ())), preferred_element_type=F32)


def split(values):
    high = values.astype(BF)
    return high, (values - high.astype(F32)).astype(BF)


def rms(values, gain):
    return values * lax.rsqrt(jnp.mean(values * values, -1, keepdims=True) + EPS) * gain


def kernel(
    sizes,
    tokens,
    gain_attn,
    qkv_fine,
    scale_fine,
    out_fine,
    gain_ffn,
    ffn_in,
    ffn_out,
    up_proj,
    gain_coarse,
    qkv_coarse,
    scale_coarse,
    out_coarse,
    pick,
    table,
    place,
    fine_o,
    coarse_o,
    tok_v,
    ga_v,
    qkv_v,
    out_v,
    gf_v,
    fin_v,
    fout_v,
    up_v,
    gc_v,
    qkvc_v,
    outc_v,
    pick_v,
    table_v,
    place_v,
    sf_s,
    sc_s,
    send_v,
    halo_v,
    tok_p,
    own_v,
    mask_v,
    part_v,
    fine_v,
    key_m,
    value_m,
    row_v,
    rows_v,
    tile_v,
    tiles_v,
    local_sem,
    halo_send,
    halo_recv,
    row_send,
    row_recv,
    tile_send,
    tile_recv,
):
    n_ha, n_wa = sizes
    n_x, n_z = n_ha // 4, n_wa // 2
    g_row, g_tile = n_z * 2, n_x * 4
    names = ("tok", "ga", "qkv", "pick", "table", "place", "sf", "out", "gf", "fin", "fout")
    names += ("up", "gc", "sc", "qkvc", "outc")
    pairs = {
        "tok": (tokens, tok_v),
        "ga": (gain_attn, ga_v),
        "pick": (pick, pick_v),
        "table": (table, table_v),
        "place": (place, place_v),
        "qkv": (qkv_fine, qkv_v),
        "sf": (scale_fine, sf_s),
        "out": (out_fine, out_v),
        "gf": (gain_ffn, gf_v),
        "fin": (ffn_in, fin_v),
        "fout": (ffn_out, fout_v),
        "up": (up_proj, up_v),
        "gc": (gain_coarse, gc_v),
        "sc": (scale_coarse, sc_s),
        "qkvc": (qkv_coarse, qkvc_v),
        "outc": (out_coarse, outc_v),
    }
    loads = {}
    for i, name in enumerate(names):
        loads[name] = pltpu.make_async_copy(*pairs[name], local_sem.at[i])
    for name in names[:4]:
        loads[name].start()
    ha, wa = lax.axis_index("ha"), lax.axis_index("wa")
    core = lax.rem(ha, 2)
    x = lax.div(ha, 4)
    z = lax.div(wa, 2)
    y = lax.rem(lax.div(ha, 2), 2) * 2 + lax.rem(wa, 2)

    def far(step, count):
        return min(step, count - step)

    def neighbour(i):
        side_r, side_c = PIECES[i][:2]
        return (lax.rem(ha - side_r + n_ha, n_ha), lax.rem(wa - side_c + n_wa, n_wa))

    def row_peer(d):
        to_z = lax.rem(z + d // 2, n_z)
        to_core = lax.rem(core + d % 2, 2)
        return (ha - core + to_core, wa - 2 * z + 2 * to_z)

    def tile_peer(d):
        to_x = lax.rem(x + d // 4, n_x)
        to_y = lax.rem(y + d % 4, 4)
        return (4 * to_x + 2 * lax.div(to_y, 2) + core, 2 * z + lax.rem(to_y, 2))

    hops = [(far(d // 2, n_z), row_peer, d) for d in range(1, g_row)]
    hops += [(far(d // 4, n_x) + far(d % 4, 4), tile_peer, d) for d in range(1, g_tile)]
    hops += [(3 if PIECES[i][0] else 2, neighbour, i) for i in range(len(PIECES))]
    hops.sort(key=lambda hop: -hop[0])
    barrier = pltpu.get_barrier_semaphore()
    where = {}
    for _, of, d in hops:
        where[of, d] = of(d)
        pl.semaphore_signal(barrier, inc=1, device_id=where[of, d], device_id_type=MESH)
    neighbours = [where[neighbour, i] for i in range(len(PIECES))]
    row_peers = [(d, where[of, d]) for _, of, d in hops if of is row_peer]
    tile_peers = [(d, where[of, d]) for _, of, d in hops if of is tile_peer]
    for name in names[4:]:
        loads[name].start()

    def spread(src, dst, send_sem, recv_sem, peers):
        for d, peer in peers:
            pltpu.make_async_remote_copy(
                src_ref=src,
                dst_ref=dst.at[d],
                send_sem=send_sem,
                recv_sem=recv_sem,
                device_id=peer,
                device_id_type=MESH,
            ).start()
        others = dst.at[pl.ds(1, len(peers))]
        return pltpu.make_async_remote_copy(
            src_ref=others,
            dst_ref=others,
            send_sem=send_sem,
            recv_sem=recv_sem,
            device_id=peers[0][1],
            device_id_type=MESH,
        )

    loads["tok"].wait()
    loads["ga"].wait()
    normed = rms(tok_v[...].astype(F32), ga_v[...]).astype(BF)
    loads["qkv"].wait()
    proj = dot(normed, qkv_v[...])
    loads["pick"].wait()
    same = pick_v[:, COUNT:]

    def head_norm(values):
        high, low = split(values * values)
        size = (dot(high, same) + dot(low, same)) * (1 / HD)
        return values * lax.rsqrt(size + EPS)

    key, value = head_norm(proj[:, C : 2 * C]).astype(BF), proj[:, 2 * C :].astype(BF)
    send_v[...] = dot(pick_v[:, :COUNT], jnp.concatenate([key, value], 1)).astype(BF)

    pl.semaphore_wait(barrier, len(hops))
    for i, (_, _, first, rows) in enumerate(PIECES):
        pltpu.make_async_remote_copy(
            src_ref=send_v.at[pl.ds(first, rows)],
            dst_ref=halo_v.at[pl.ds(first, rows)],
            send_sem=halo_send,
            recv_sem=halo_recv,
            device_id=neighbours[i],
            device_id_type=MESH,
        ).start()
    halos = pltpu.make_async_remote_copy(
        src_ref=send_v,
        dst_ref=halo_v,
        send_sem=halo_send,
        recv_sem=halo_recv,
        device_id=neighbours[0],
        device_id_type=MESH,
    )

    loads["table"].wait()
    loads["place"].wait()
    loads["sf"].wait()
    perm = table_v[:, :COUNT]
    tok_p[...] = dot(perm, tok_v[...]).astype(BF)
    lane_head = lax.broadcasted_iota(jnp.int32, (COUNT, C), 1) // HD
    scales = jnp.zeros((1, C), F32)
    for h in range(HEADS):
        scales = jnp.where(lane_head[0:1] == h, sf_s[h] * (LOG2E / HD), scales)
    query = dot(perm, (head_norm(proj[:, :C]) * scales).astype(BF)).astype(BF)
    zero, one = jnp.zeros((COUNT, C), BF), jnp.ones((COUNT, C), BF)
    queries = [jnp.where(lane_head == h, query, zero) for h in range(HEADS)]

    key_row = place_v[0:1, :] + ha * SIDE
    key_col = place_v[1:2, :] + wa * SIDE
    inside = (
        (key_row >= 0) & (key_row < SIDE * n_ha) & (key_col >= 0) & (key_col < SIDE * n_wa)
    ).astype(F32)
    mask_v[...] = table_v[:EDGE, 3 * COUNT : 4 * COUNT].astype(F32) * inside

    def attend(rows, keys, value, mask):
        sums = []
        for first in range(2):
            weights, values = [], []
            for h in range(first, HEADS, 2):
                raw = dot_t(queries[h][:rows], keys)
                weights.append((jnp.exp2(raw) * mask).astype(BF))
                count = jnp.where(lane_head == h + 1 - 2 * first, one, zero)
                values.append(jnp.where(lane_head == h, value, count))
            sums.append(dot(jnp.concatenate(weights, 1), jnp.concatenate(values, 0)))
        return sums

    def finished(sum_a, sum_b, tok):
        even = lax.rem(lane_head[: tok.shape[0]], 2) == 0
        over = jnp.where(even, sum_a, sum_b)
        under = jnp.where(even, sum_b, sum_a)
        under = jnp.concatenate(
            [pltpu.roll(under[:, :LANES], HD, 1), pltpu.roll(under[:, LANES:], HD, 1)], 1
        )
        attn = (over / under).astype(BF)
        h1 = (tok.astype(F32) + dot(attn, out_v[...])).astype(BF)
        h1 = h1.astype(F32)
        n2 = rms(h1, gf_v[...]).astype(BF)
        acc = 0.0
        for part in range(FFH // C):
            gate = dot(n2, fin_v[:, part * C : (part + 1) * C])
            lift = dot(n2, fin_v[:, FFH + part * C : FFH + (part + 1) * C])
            bend = jnp.tanh(gate * (GELU + (GELU * 0.044715) * (gate * gate)))
            gated = (gate * lift * (1.0 + bend)).astype(BF)
            acc = acc + dot(gated, fout_v[part * C : (part + 1) * C, :])
        return (h1 + 0.5 * acc).astype(BF)

    own_mask = table_v[:, 2 * COUNT : 3 * COUNT].astype(F32)
    sum_a, sum_b = attend(COUNT, key, value, own_mask)
    own_v[0] = sum_a[:EDGE]
    own_v[1] = sum_b[:EDGE]
    for name in ("out", "gf", "fin", "fout"):
        loads[name].wait()
    fine = finished(sum_a[EDGE:], sum_b[EDGE:], tok_p[EDGE:, :])
    fine_v[EDGE:, :] = fine
    part_v[...] = jnp.sum(fine.astype(F32), 0, keepdims=True)

    for name in ("up", "gc", "qkvc"):
        loads[name].wait()
    up_high, up_low = split(up_v[...].astype(F32) * gc_v[...])

    def through(part):
        after = qkvc_v[:, part * CC : (part + 1) * CC]
        return (dot(up_high, after) + dot(up_low, after)).astype(BF)

    key_m[...] = through(1)

    halos.wait_recv()
    sum_a, sum_b = attend(EDGE, halo_v[:, :C], halo_v[:, C:], mask_v[...])
    fine = finished(own_v[0] + sum_a, own_v[1] + sum_b, tok_p[:EDGE, :])
    fine_v[:EDGE, :] = fine
    pooled = part_v[...] + jnp.sum(fine.astype(F32), 0, keepdims=True)
    pooled = (pooled * (1 / COUNT)).astype(BF)

    row = pooled.astype(F32)
    loads["sc"].wait()
    own = jnp.broadcast_to(row, (HEADS_C, C)).astype(BF)
    coarse_own = dot(own, up_v[...]).astype(BF)
    coarse_f = coarse_own.astype(F32)
    factor = lax.rsqrt(jnp.mean(coarse_f * coarse_f, -1, keepdims=True) + EPS)
    head_of_row = lax.broadcasted_iota(jnp.int32, (HEADS_C, CC), 0)
    diag = head_of_row == lax.broadcasted_iota(jnp.int32, (HEADS_C, CC), 1) // HD

    def norm_of(values):
        return lax.rsqrt(jnp.sum(values * values, -1, keepdims=True) * (1 / HD) + EPS)

    ck = jnp.where(diag, dot(own, key_m[...]), 0.0) * factor
    slot = lax.broadcasted_iota(jnp.int32, (HEADS_C, LANES), 0)
    lane = lax.broadcasted_iota(jnp.int32, (HEADS_C, LANES), 1)
    scales = jnp.zeros((HEADS_C, 1), F32)
    for h in range(HEADS_C):
        scales = jnp.where(slot[:, 0:1] == h, sc_s[h] * (LOG2E / HD), scales)
    norms = norm_of(ck) * factor * scales
    twice = lax.rem(lane, LANES // 2)
    norms = jnp.sum(jnp.where(slot == twice, norms, 0.0), 0, keepdims=True)
    norms = jnp.where(twice[0:1] == HEADS_C, factor[0:1], norms)
    high, low = split(norms)
    norms = jnp.where(lane[0:1] < LANES // 2, high.astype(F32), low.astype(F32))
    row = jnp.concatenate([row, norms], 1)

    row_v[...] = row
    rows = spread(row_v, rows_v, row_send, row_recv, row_peers)
    fine_o[...] = dot(table_v[:, COUNT : 2 * COUNT], fine_v[...]).astype(BF)

    nc_own = (coarse_f * factor * gc_v[...]).astype(BF)
    cq = jnp.where(diag, dot(nc_own, qkvc_v[:, :CC]), 0.0)
    cq = (cq * norm_of(cq)).astype(BF)

    back = jnp.concatenate(split(dot_t(cq, key_m[...])), 1)

    rows.wait_recv()
    at = lax.broadcasted_iota(jnp.int32, (g_row, C + LANES), 0)
    tile = jnp.broadcast_to(row, (g_row, C + LANES))
    for d in range(1, g_row):
        tile = jnp.where(at == d, rows_v[d], tile)
    tile = tile.astype(BF)
    tile_v[...] = tile
    tiles = spread(tile_v, tiles_v, tile_send, tile_recv, tile_peers)
    tiles_v[0] = tile

    value_m[...] = through(2)

    tiles.wait_recv()
    every = tiles_v[...].reshape(g_tile * g_row, C + LANES)
    norms = every[:, C:].astype(F32).T
    norms = norms[: LANES // 2] + norms[LANES // 2 :]
    every = every[:, :C]
    scores = dot_t(back, jnp.concatenate([every, every], 1))
    cexp = jnp.exp2(scores * norms[:HEADS_C])
    rest = 1 / jnp.sum(cexp, -1, keepdims=True)
    cexp = cexp * norms[HEADS_C : HEADS_C + 1]
    mixed = dot(jnp.concatenate(split(cexp), 0), every)
    mixed = (mixed[:HEADS_C] + mixed[HEADS_C:]) * rest
    mixed = dot(jnp.concatenate(split(mixed), 0), value_m[...])
    cattn = jnp.where(diag, mixed[:HEADS_C] + mixed[HEADS_C:], 0.0)
    cattn = jnp.sum(cattn, 0, keepdims=True)
    loads["outc"].wait()
    cattn = jnp.broadcast_to(cattn, (HEADS_C, CC)).astype(BF)
    result = coarse_f + dot(cattn, outc_v[...])
    coarse_o[...] = result[0:1].astype(BF)

    for copy in (halos, rows, tiles):
        copy.wait_send()


def finish(fine, coarse, fine_o, coarse_o, sem):
    copies = [
        pltpu.make_async_copy(fine, fine_o, sem.at[0]),
        pltpu.make_async_copy(coarse, coarse_o, sem.at[1]),
    ]
    for copy in copies:
        copy.start()
    for copy in copies:
        copy.wait()


def solution(mesh):
    sizes = (mesh.shape["ha"], mesh.shape["wa"])
    g_row, g_tile = sizes[1], sizes[0]
    pick, table, place = tables()
    pick, table = jnp.asarray(pick, BF), jnp.asarray(table, BF)
    place = jnp.asarray(place)

    def shards(
        tokens,
        gain_attn,
        qkv_fine,
        scale_fine,
        out_fine,
        gain_ffn,
        ffn_in,
        ffn_out,
        up_proj,
        gain_coarse,
        qkv_coarse,
        scale_coarse,
        out_coarse,
    ):
        hbm = pl.BlockSpec(memory_space=pl.ANY)
        fine, coarse = pl.pallas_call(
            functools.partial(kernel, sizes),
            out_shape=(pltpu.VMEM((COUNT, C), BF), pltpu.VMEM((1, CC), BF)),
            in_specs=[hbm] * 16,
            out_specs=(pl.BlockSpec(memory_space=pltpu.VMEM),) * 2,
            scratch_shapes=[
                pltpu.VMEM((COUNT, C), BF),
                pltpu.VMEM((1, C), F32),
                pltpu.VMEM((C, 3 * C), BF),
                pltpu.VMEM((C, C), BF),
                pltpu.VMEM((1, C), F32),
                pltpu.VMEM((C, 2 * FFH), BF),
                pltpu.VMEM((FFH, C), BF),
                pltpu.VMEM((C, CC), BF),
                pltpu.VMEM((1, CC), F32),
                pltpu.VMEM((CC, 3 * CC), BF),
                pltpu.VMEM((CC, CC), BF),
                pltpu.VMEM((COUNT, 2 * COUNT), BF),
                pltpu.VMEM((COUNT, 4 * COUNT), BF),
                pltpu.VMEM((8, COUNT), jnp.int32),
                pltpu.SMEM((HEADS,), F32),
                pltpu.SMEM((HEADS_C,), F32),
                pltpu.VMEM((COUNT, 2 * C), BF),
                pltpu.VMEM((COUNT, 2 * C), BF),
                pltpu.VMEM((COUNT, C), BF),
                pltpu.VMEM((2, EDGE, C), F32),
                pltpu.VMEM((EDGE, COUNT), F32),
                pltpu.VMEM((1, C), F32),
                pltpu.VMEM((COUNT, C), BF),
                pltpu.VMEM((C, CC), BF),
                pltpu.VMEM((C, CC), BF),
                pltpu.VMEM((1, C + LANES), F32),
                pltpu.VMEM((g_row, 1, C + LANES), F32),
                pltpu.VMEM((g_row, C + LANES), BF),
                pltpu.VMEM((g_tile, g_row, C + LANES), BF),
                pltpu.SemaphoreType.DMA((16,)),
                *[pltpu.SemaphoreType.DMA] * 6,
            ],
            compiler_params=pltpu.CompilerParams(
                collective_id=0, has_side_effects=True, vmem_limit_bytes=VMEM
            ),
        )(*[pltpu.with_memory_space_constraint(v, pltpu.HBM) for v in (
            tokens.reshape(COUNT, C),
            gain_attn.reshape(1, C),
            qkv_fine,
            scale_fine,
            out_fine,
            gain_ffn.reshape(1, C),
            ffn_in,
            ffn_out,
            up_proj,
            gain_coarse.reshape(1, CC),
            qkv_coarse,
            scale_coarse,
            out_coarse,
            pick,
            table,
            place,
        )])
        fine, coarse = pl.pallas_call(
            finish,
            out_shape=(
                jax.ShapeDtypeStruct((COUNT, C), BF),
                jax.ShapeDtypeStruct((1, CC), BF),
            ),
            in_specs=[pl.BlockSpec(memory_space=pltpu.VMEM)] * 2,
            out_specs=(pl.BlockSpec(memory_space=pltpu.HBM),) * 2,
            scratch_shapes=[pltpu.SemaphoreType.DMA((2,))],
            compiler_params=pltpu.CompilerParams(vmem_limit_bytes=1024 * 1024),
        )(fine, coarse)
        return fine.reshape(SIDE, SIDE, C), coarse.reshape(1, 1, CC)

    return jax.shard_map(
        shards,
        mesh=mesh,
        in_specs=(P("ha", "wa", None),) + (P(),) * 12,
        out_specs=(P("ha", "wa", None), P("ha", "wa", None)),
        check_vma=False,
    )
```

```python
import functools

import jax
import jax.numpy as jnp
import numpy as np
from jax import lax
from jax.experimental import pallas as pl
from jax.experimental.pallas import tpu as pltpu
from jax.sharding import PartitionSpec as P

C = 256
CC = 1024
HD = 64
FFH = 768
RADIUS = 3
SIDE = 16
COUNT = SIDE * SIDE
EDGE = 160
HEADS = 4
HEADS_C = 16
LANES = 128
EPS = 1e-06
VMEM = 40 * 1024 * 1024
LOG2E = 1.4426950408889634
GELU = 0.7978845608028654
MESH = pl.DeviceIdType.MESH
BF = jnp.bfloat16
F32 = jnp.float32

PIECES = (
    (-1, 0, 0, 48),
    (1, 0, 48, 48),
    (0, -1, 96, 48),
    (0, 1, 144, 48),
    (-1, -1, 192, 16),
    (-1, 1, 208, 16),
    (1, -1, 224, 16),
    (1, 1, 240, 16),
)


def tables():
    span = {-1: range(SIDE - RADIUS, SIDE), 0: range(SIDE), 1: range(RADIUS)}
    pick = np.zeros((COUNT, COUNT))
    row = np.full((COUNT,), -100, np.int32)
    col = np.full((COUNT,), -100, np.int32)
    for side_r, side_c, first, _ in PIECES:
        at = first
        for r in span[side_r]:
            for c in span[side_c]:
                pick[at, r * SIDE + c] = 1
                row[at] = r + SIDE * side_r
                col[at] = c + SIDE * side_c
                at += 1
    natural = np.arange(COUNT)
    own_r, own_c = natural // SIDE, natural % SIDE
    inner = np.minimum(
        np.minimum(own_r, SIDE - 1 - own_r), np.minimum(own_c, SIDE - 1 - own_c)
    )
    order = np.argsort(inner, kind="stable")
    perm = np.eye(COUNT)[order]
    own_r, own_c = own_r[order][:, None], own_c[order][:, None]

    def near(key_r, key_c):
        return (np.abs(key_r - own_r) <= RADIUS) & (np.abs(key_c - own_c) <= RADIUS)

    heads = (natural[:, None] // HD) == (natural[None] // HD)
    parts = [perm, perm.T, near(natural // SIDE, natural % SIDE), near(row[None], col[None])]
    place = np.zeros((8, COUNT), np.int32)
    place[0], place[1] = row, col
    return np.concatenate([pick, heads], 1), np.concatenate(parts, 1), place


def dot(a, b):
    return jnp.dot(a, b, preferred_element_type=F32)


def dot_t(a, b):
    return lax.dot_general(a, b, (((1,), (1,)), ((), ())), preferred_element_type=F32)


def split(values):
    high = values.astype(BF)
    return high, (values - high.astype(F32)).astype(BF)


def rms(values, gain):
    return values * lax.rsqrt(jnp.mean(values * values, -1, keepdims=True) + EPS) * gain


def kernel(
    sizes,
    tokens,
    gain_attn,
    qkv_fine,
    scale_fine,
    out_fine,
    gain_ffn,
    ffn_in,
    ffn_out,
    up_proj,
    gain_coarse,
    qkv_coarse,
    scale_coarse,
    out_coarse,
    pick,
    table,
    place,
    fine_o,
    coarse_o,
    tok_v,
    ga_v,
    qkv_v,
    out_v,
    gf_v,
    fin_v,
    fout_v,
    up_v,
    gc_v,
    qkvc_v,
    outc_v,
    pick_v,
    table_v,
    place_v,
    sf_s,
    sc_s,
    send_v,
    halo_v,
    tok_p,
    own_v,
    mask_v,
    part_v,
    fine_v,
    key_m,
    value_m,
    row_v,
    rows_v,
    tile_v,
    tiles_v,
    local_sem,
    halo_send,
    halo_recv,
    row_send,
    row_recv,
    tile_send,
    tile_recv,
):
    n_ha, n_wa = sizes
    n_x, n_z = n_ha // 4, n_wa // 2
    g_row, g_tile = n_z * 2, n_x * 4
    names = ("tok", "ga", "qkv", "pick", "table", "place", "sf", "out", "gf", "fin", "fout")
    names += ("up", "gc", "sc", "qkvc", "outc")
    pairs = {
        "tok": (tokens, tok_v),
        "ga": (gain_attn, ga_v),
        "pick": (pick, pick_v),
        "table": (table, table_v),
        "place": (place, place_v),
        "qkv": (qkv_fine, qkv_v),
        "sf": (scale_fine, sf_s),
        "out": (out_fine, out_v),
        "gf": (gain_ffn, gf_v),
        "fin": (ffn_in, fin_v),
        "fout": (ffn_out, fout_v),
        "up": (up_proj, up_v),
        "gc": (gain_coarse, gc_v),
        "sc": (scale_coarse, sc_s),
        "qkvc": (qkv_coarse, qkvc_v),
        "outc": (out_coarse, outc_v),
    }
    loads = {}
    for i, name in enumerate(names):
        loads[name] = pltpu.make_async_copy(*pairs[name], local_sem.at[i])
    for name in names[:4]:
        loads[name].start()
    ha, wa = lax.axis_index("ha"), lax.axis_index("wa")
    core = lax.rem(ha, 2)
    x = lax.div(ha, 4)
    z = lax.div(wa, 2)
    y = lax.rem(lax.div(ha, 2), 2) * 2 + lax.rem(wa, 2)

    def far(step, count):
        return min(step, count - step)

    def neighbour(i):
        side_r, side_c = PIECES[i][:2]
        return (lax.rem(ha - side_r + n_ha, n_ha), lax.rem(wa - side_c + n_wa, n_wa))

    def row_peer(d):
        to_z = lax.rem(z + d // 2, n_z)
        to_core = lax.rem(core + d % 2, 2)
        return (ha - core + to_core, wa - 2 * z + 2 * to_z)

    def tile_peer(d):
        to_x = lax.rem(x + d // 4, n_x)
        to_y = lax.rem(y + d % 4, 4)
        return (4 * to_x + 2 * lax.div(to_y, 2) + core, 2 * z + lax.rem(to_y, 2))

    hops = [(far(d // 2, n_z), row_peer, d) for d in range(1, g_row)]
    hops += [(far(d // 4, n_x) + far(d % 4, 4), tile_peer, d) for d in range(1, g_tile)]
    hops += [(3 if PIECES[i][0] else 2, neighbour, i) for i in range(len(PIECES))]
    hops.sort(key=lambda hop: -hop[0])
    barrier = pltpu.get_barrier_semaphore()
    where = {}
    for _, of, d in hops:
        where[of, d] = of(d)
        pl.semaphore_signal(barrier, inc=1, device_id=where[of, d], device_id_type=MESH)
    neighbours = [where[neighbour, i] for i in range(len(PIECES))]
    row_peers = [(d, where[of, d]) for _, of, d in hops if of is row_peer]
    tile_peers = [(d, where[of, d]) for _, of, d in hops if of is tile_peer]
    for name in names[4:]:
        loads[name].start()

    def spread(src, dst, send_sem, recv_sem, peers):
        for d, peer in peers:
            pltpu.make_async_remote_copy(
                src_ref=src,
                dst_ref=dst.at[d],
                send_sem=send_sem,
                recv_sem=recv_sem,
                device_id=peer,
                device_id_type=MESH,
            ).start()
        others = dst.at[pl.ds(1, len(peers))]
        return pltpu.make_async_remote_copy(
            src_ref=others,
            dst_ref=others,
            send_sem=send_sem,
            recv_sem=recv_sem,
            device_id=peers[0][1],
            device_id_type=MESH,
        )

    loads["tok"].wait()
    loads["ga"].wait()
    normed = rms(tok_v[...].astype(F32), ga_v[...]).astype(BF)
    loads["qkv"].wait()
    proj = dot(normed, qkv_v[...])
    loads["pick"].wait()
    same = pick_v[:, COUNT:]

    def head_norm(values):
        high, low = split(values * values)
        size = (dot(high, same) + dot(low, same)) * (1 / HD)
        return values * lax.rsqrt(size + EPS)

    key, value = head_norm(proj[:, C : 2 * C]).astype(BF), proj[:, 2 * C :].astype(BF)
    send_v[...] = dot(pick_v[:, :COUNT], jnp.concatenate([key, value], 1)).astype(BF)

    pl.semaphore_wait(barrier, len(hops))
    for i, (_, _, first, rows) in enumerate(PIECES):
        pltpu.make_async_remote_copy(
            src_ref=send_v.at[pl.ds(first, rows)],
            dst_ref=halo_v.at[pl.ds(first, rows)],
            send_sem=halo_send,
            recv_sem=halo_recv,
            device_id=neighbours[i],
            device_id_type=MESH,
        ).start()
    halos = pltpu.make_async_remote_copy(
        src_ref=send_v,
        dst_ref=halo_v,
        send_sem=halo_send,
        recv_sem=halo_recv,
        device_id=neighbours[0],
        device_id_type=MESH,
    )

    loads["table"].wait()
    loads["place"].wait()
    loads["sf"].wait()
    perm = table_v[:, :COUNT]
    tok_p[...] = dot(perm, tok_v[...]).astype(BF)
    lane_head = lax.broadcasted_iota(jnp.int32, (COUNT, C), 1) // HD
    scales = jnp.zeros((1, C), F32)
    for h in range(HEADS):
        scales = jnp.where(lane_head[0:1] == h, sf_s[h] * (LOG2E / HD), scales)
    query = dot(perm, (head_norm(proj[:, :C]) * scales).astype(BF)).astype(BF)
    zero, one = jnp.zeros((COUNT, C), BF), jnp.ones((COUNT, C), BF)
    queries = [jnp.where(lane_head == h, query, zero) for h in range(HEADS)]

    key_row = place_v[0:1, :] + ha * SIDE
    key_col = place_v[1:2, :] + wa * SIDE
    inside = (
        (key_row >= 0) & (key_row < SIDE * n_ha) & (key_col >= 0) & (key_col < SIDE * n_wa)
    ).astype(F32)
    mask_v[...] = table_v[:EDGE, 3 * COUNT : 4 * COUNT].astype(F32) * inside

    def attend(rows, keys, value, mask):
        sums = [0.0, 0.0]
        for h in range(HEADS):
            raw = dot_t(queries[h][:rows], keys)
            weights = (jnp.exp2(raw) * mask).astype(BF)
            count = jnp.where(lane_head == h + 1 - 2 * (h % 2), one, zero)
            sums[h % 2] += dot(weights, jnp.where(lane_head == h, value, count))
        return sums

    def finished(sum_a, sum_b, tok):
        even = lax.rem(lane_head[: tok.shape[0]], 2) == 0
        over = jnp.where(even, sum_a, sum_b)
        under = jnp.where(even, sum_b, sum_a)
        under = jnp.concatenate(
            [pltpu.roll(under[:, :LANES], HD, 1), pltpu.roll(under[:, LANES:], HD, 1)], 1
        )
        attn = (over / under).astype(BF)
        h1 = (tok.astype(F32) + dot(attn, out_v[...])).astype(BF)
        h1 = h1.astype(F32)
        n2 = rms(h1, gf_v[...]).astype(BF)
        acc = 0.0
        for part in range(FFH // C):
            gate = dot(n2, fin_v[:, part * C : (part + 1) * C])
            lift = dot(n2, fin_v[:, FFH + part * C : FFH + (part + 1) * C])
            bend = jnp.tanh(gate * (GELU + (GELU * 0.044715) * (gate * gate)))
            gated = (gate * lift * (1.0 + bend)).astype(BF)
            acc = acc + dot(gated, fout_v[part * C : (part + 1) * C, :])
        return (h1 + 0.5 * acc).astype(BF)

    own_mask = table_v[:, 2 * COUNT : 3 * COUNT].astype(F32)
    sum_a, sum_b = attend(COUNT, key, value, own_mask)
    own_v[0] = sum_a[:EDGE]
    own_v[1] = sum_b[:EDGE]
    for name in ("out", "gf", "fin", "fout"):
        loads[name].wait()
    fine = finished(sum_a[EDGE:], sum_b[EDGE:], tok_p[EDGE:, :])
    fine_v[EDGE:, :] = fine
    part_v[...] = jnp.sum(fine.astype(F32), 0, keepdims=True)

    for name in ("up", "gc", "qkvc"):
        loads[name].wait()
    up_high, up_low = split(up_v[...].astype(F32) * gc_v[...])

    def through(part):
        after = qkvc_v[:, part * CC : (part + 1) * CC]
        return (dot(up_high, after) + dot(up_low, after)).astype(BF)

    key_m[...] = through(1)

    halos.wait_recv()
    sum_a, sum_b = attend(EDGE, halo_v[:, :C], halo_v[:, C:], mask_v[...])
    fine = finished(own_v[0] + sum_a, own_v[1] + sum_b, tok_p[:EDGE, :])
    fine_v[:EDGE, :] = fine
    pooled = part_v[...] + jnp.sum(fine.astype(F32), 0, keepdims=True)
    pooled = (pooled * (1 / COUNT)).astype(BF)

    row = pooled.astype(F32)
    loads["sc"].wait()
    own = jnp.broadcast_to(row, (HEADS_C, C)).astype(BF)
    coarse_own = dot(own, up_v[...]).astype(BF)
    coarse_f = coarse_own.astype(F32)
    factor = lax.rsqrt(jnp.mean(coarse_f * coarse_f, -1, keepdims=True) + EPS)
    head_of_row = lax.broadcasted_iota(jnp.int32, (HEADS_C, CC), 0)
    diag = head_of_row == lax.broadcasted_iota(jnp.int32, (HEADS_C, CC), 1) // HD

    def norm_of(values):
        return lax.rsqrt(jnp.sum(values * values, -1, keepdims=True) * (1 / HD) + EPS)

    ck = jnp.where(diag, dot(own, key_m[...]), 0.0) * factor
    slot = lax.broadcasted_iota(jnp.int32, (HEADS_C, LANES), 0)
    lane = lax.broadcasted_iota(jnp.int32, (HEADS_C, LANES), 1)
    scales = jnp.zeros((HEADS_C, 1), F32)
    for h in range(HEADS_C):
        scales = jnp.where(slot[:, 0:1] == h, sc_s[h] * (LOG2E / HD), scales)
    norms = norm_of(ck) * factor * scales
    twice = lax.rem(lane, LANES // 2)
    norms = jnp.sum(jnp.where(slot == twice, norms, 0.0), 0, keepdims=True)
    norms = jnp.where(twice[0:1] == HEADS_C, factor[0:1], norms)
    high, low = split(norms)
    norms = jnp.where(lane[0:1] < LANES // 2, high.astype(F32), low.astype(F32))
    row = jnp.concatenate([row, norms], 1)

    row_v[...] = row
    rows = spread(row_v, rows_v, row_send, row_recv, row_peers)
    fine_o[...] = dot(table_v[:, COUNT : 2 * COUNT], fine_v[...]).astype(BF)

    nc_own = (coarse_f * factor * gc_v[...]).astype(BF)
    cq = jnp.where(diag, dot(nc_own, qkvc_v[:, :CC]), 0.0)
    cq = (cq * norm_of(cq)).astype(BF)

    back = jnp.concatenate(split(dot_t(cq, key_m[...])), 1)

    rows.wait_recv()
    at = lax.broadcasted_iota(jnp.int32, (g_row, C + LANES), 0)
    tile = jnp.broadcast_to(row, (g_row, C + LANES))
    for d in range(1, g_row):
        tile = jnp.where(at == d, rows_v[d], tile)
    tile = tile.astype(BF)
    tile_v[...] = tile
    tiles = spread(tile_v, tiles_v, tile_send, tile_recv, tile_peers)
    tiles_v[0] = tile

    value_m[...] = through(2)

    tiles.wait_recv()
    every = tiles_v[...].reshape(g_tile * g_row, C + LANES)
    norms = every[:, C:].astype(F32).T
    norms = norms[: LANES // 2] + norms[LANES // 2 :]
    every = every[:, :C]
    scores = dot_t(back, jnp.concatenate([every, every], 1))
    cexp = jnp.exp2(scores * norms[:HEADS_C])
    rest = 1 / jnp.sum(cexp, -1, keepdims=True)
    cexp = cexp * norms[HEADS_C : HEADS_C + 1]
    mixed = dot(jnp.concatenate(split(cexp), 0), every)
    mixed = (mixed[:HEADS_C] + mixed[HEADS_C:]) * rest
    mixed = dot(jnp.concatenate(split(mixed), 0), value_m[...])
    cattn = jnp.where(diag, mixed[:HEADS_C] + mixed[HEADS_C:], 0.0)
    cattn = jnp.sum(cattn, 0, keepdims=True)
    loads["outc"].wait()
    cattn = jnp.broadcast_to(cattn, (HEADS_C, CC)).astype(BF)
    result = coarse_f
    for first in range(0, CC, C):
        result = result + dot(cattn[:, first : first + C], outc_v[first : first + C, :])
    coarse_o[...] = result[0:1].astype(BF)

    for copy in (halos, rows, tiles):
        copy.wait_send()


def finish(fine, coarse, fine_o, coarse_o, sem):
    copies = [
        pltpu.make_async_copy(fine, fine_o, sem.at[0]),
        pltpu.make_async_copy(coarse, coarse_o, sem.at[1]),
    ]
    for copy in copies:
        copy.start()
    for copy in copies:
        copy.wait()


def solution(mesh):
    sizes = (mesh.shape["ha"], mesh.shape["wa"])
    g_row, g_tile = sizes[1], sizes[0]
    pick, table, place = tables()
    pick, table = jnp.asarray(pick, BF), jnp.asarray(table, BF)
    place = jnp.asarray(place)

    def shards(
        tokens,
        gain_attn,
        qkv_fine,
        scale_fine,
        out_fine,
        gain_ffn,
        ffn_in,
        ffn_out,
        up_proj,
        gain_coarse,
        qkv_coarse,
        scale_coarse,
        out_coarse,
    ):
        hbm = pl.BlockSpec(memory_space=pl.ANY)
        fine, coarse = pl.pallas_call(
            functools.partial(kernel, sizes),
            out_shape=(pltpu.VMEM((COUNT, C), BF), pltpu.VMEM((1, CC), BF)),
            in_specs=[hbm] * 16,
            out_specs=(pl.BlockSpec(memory_space=pltpu.VMEM),) * 2,
            scratch_shapes=[
                pltpu.VMEM((COUNT, C), BF),
                pltpu.VMEM((1, C), F32),
                pltpu.VMEM((C, 3 * C), BF),
                pltpu.VMEM((C, C), BF),
                pltpu.VMEM((1, C), F32),
                pltpu.VMEM((C, 2 * FFH), BF),
                pltpu.VMEM((FFH, C), BF),
                pltpu.VMEM((C, CC), BF),
                pltpu.VMEM((1, CC), F32),
                pltpu.VMEM((CC, 3 * CC), BF),
                pltpu.VMEM((CC, CC), BF),
                pltpu.VMEM((COUNT, 2 * COUNT), BF),
                pltpu.VMEM((COUNT, 4 * COUNT), BF),
                pltpu.VMEM((8, COUNT), jnp.int32),
                pltpu.SMEM((HEADS,), F32),
                pltpu.SMEM((HEADS_C,), F32),
                pltpu.VMEM((COUNT, 2 * C), BF),
                pltpu.VMEM((COUNT, 2 * C), BF),
                pltpu.VMEM((COUNT, C), BF),
                pltpu.VMEM((2, EDGE, C), F32),
                pltpu.VMEM((EDGE, COUNT), F32),
                pltpu.VMEM((1, C), F32),
                pltpu.VMEM((COUNT, C), BF),
                pltpu.VMEM((C, CC), BF),
                pltpu.VMEM((C, CC), BF),
                pltpu.VMEM((1, C + LANES), F32),
                pltpu.VMEM((g_row, 1, C + LANES), F32),
                pltpu.VMEM((g_row, C + LANES), BF),
                pltpu.VMEM((g_tile, g_row, C + LANES), BF),
                pltpu.SemaphoreType.DMA((16,)),
                *[pltpu.SemaphoreType.DMA] * 6,
            ],
            compiler_params=pltpu.CompilerParams(
                collective_id=0, has_side_effects=True, vmem_limit_bytes=VMEM
            ),
        )(*[pltpu.with_memory_space_constraint(v, pltpu.HBM) for v in (
            tokens.reshape(COUNT, C),
            gain_attn.reshape(1, C),
            qkv_fine,
            scale_fine,
            out_fine,
            gain_ffn.reshape(1, C),
            ffn_in,
            ffn_out,
            up_proj,
            gain_coarse.reshape(1, CC),
            qkv_coarse,
            scale_coarse,
            out_coarse,
            pick,
            table,
            place,
        )])
        fine, coarse = pl.pallas_call(
            finish,
            out_shape=(
                jax.ShapeDtypeStruct((COUNT, C), BF),
                jax.ShapeDtypeStruct((1, CC), BF),
            ),
            in_specs=[pl.BlockSpec(memory_space=pltpu.VMEM)] * 2,
            out_specs=(pl.BlockSpec(memory_space=pltpu.HBM),) * 2,
            scratch_shapes=[pltpu.SemaphoreType.DMA((2,))],
            compiler_params=pltpu.CompilerParams(vmem_limit_bytes=1024 * 1024),
        )(fine, coarse)
        return fine.reshape(SIDE, SIDE, C), coarse.reshape(1, 1, CC)

    return jax.shard_map(
        shards,
        mesh=mesh,
        in_specs=(P("ha", "wa", None),) + (P(),) * 12,
        out_specs=(P("ha", "wa", None), P("ha", "wa", None)),
        check_vma=False,
    )
```

```python
import functools

import jax
import jax.numpy as jnp
import numpy as np
from jax import lax
from jax.experimental import pallas as pl
from jax.experimental.pallas import tpu as pltpu
from jax.sharding import PartitionSpec as P

C = 256
CC = 1024
HD = 64
FFH = 768
RADIUS = 3
SIDE = 16
COUNT = SIDE * SIDE
EDGE = 160
HEADS = 4
HEADS_C = 16
LANES = 128
EPS = 1e-06
VMEM = 40 * 1024 * 1024
LOG2E = 1.4426950408889634
GELU = 0.7978845608028654
MESH = pl.DeviceIdType.MESH
BF = jnp.bfloat16
F32 = jnp.float32

PIECES = (
    (-1, 0, 0, 48),
    (1, 0, 48, 48),
    (0, -1, 96, 48),
    (0, 1, 144, 48),
    (-1, -1, 192, 16),
    (-1, 1, 208, 16),
    (1, -1, 224, 16),
    (1, 1, 240, 16),
)


def tables():
    span = {-1: range(SIDE - RADIUS, SIDE), 0: range(SIDE), 1: range(RADIUS)}
    pick = np.zeros((COUNT, COUNT))
    row = np.full((COUNT,), -100, np.int32)
    col = np.full((COUNT,), -100, np.int32)
    for side_r, side_c, first, _ in PIECES:
        at = first
        for r in span[side_r]:
            for c in span[side_c]:
                pick[at, r * SIDE + c] = 1
                row[at] = r + SIDE * side_r
                col[at] = c + SIDE * side_c
                at += 1
    natural = np.arange(COUNT)
    own_r, own_c = natural // SIDE, natural % SIDE
    inner = np.minimum(
        np.minimum(own_r, SIDE - 1 - own_r), np.minimum(own_c, SIDE - 1 - own_c)
    )
    order = np.argsort(inner, kind="stable")
    perm = np.eye(COUNT)[order]
    own_r, own_c = own_r[order][:, None], own_c[order][:, None]

    def near(key_r, key_c):
        return (np.abs(key_r - own_r) <= RADIUS) & (np.abs(key_c - own_c) <= RADIUS)

    heads = (natural[:, None] // HD) == (natural[None] // HD)
    parts = [perm, perm.T, near(natural // SIDE, natural % SIDE), near(row[None], col[None])]
    place = np.zeros((8, COUNT), np.int32)
    place[0], place[1] = row, col
    return np.concatenate([pick, heads], 1), np.concatenate(parts, 1), place


def dot(a, b):
    return jnp.dot(a, b, preferred_element_type=F32)


def dot_t(a, b):
    return lax.dot_general(a, b, (((1,), (1,)), ((), ())), preferred_element_type=F32)


def split(values):
    high = values.astype(BF)
    return high, (values - high.astype(F32)).astype(BF)


def rms(values, gain):
    return values * lax.rsqrt(jnp.mean(values * values, -1, keepdims=True) + EPS) * gain


def kernel(
    sizes,
    tokens,
    gain_attn,
    qkv_fine,
    scale_fine,
    out_fine,
    gain_ffn,
    ffn_in,
    ffn_out,
    up_proj,
    gain_coarse,
    qkv_coarse,
    scale_coarse,
    out_coarse,
    pick,
    table,
    place,
    fine_o,
    coarse_o,
    tok_v,
    ga_v,
    qkv_v,
    out_v,
    gf_v,
    fin_v,
    fout_v,
    up_v,
    gc_v,
    qkvc_v,
    outc_v,
    pick_v,
    table_v,
    place_v,
    sf_s,
    sc_s,
    send_v,
    halo_v,
    tok_p,
    own_v,
    mask_v,
    part_v,
    fine_v,
    key_m,
    value_m,
    row_v,
    rows_v,
    tile_v,
    tiles_v,
    local_sem,
    halo_send,
    halo_recv,
    row_send,
    row_recv,
    tile_send,
    tile_recv,
):
    n_ha, n_wa = sizes
    n_x, n_z = n_ha // 4, n_wa // 2
    g_row, g_tile = n_z * 2, n_x * 4
    names = ("tok", "ga", "qkv", "pick", "table", "place", "sf", "sc", "out", "gf", "fin", "fout")
    again = ("up", "gc", "qkvc", "outc")
    pairs = {
        "tok": (tokens, tok_v),
        "ga": (gain_attn, ga_v),
        "pick": (pick, pick_v),
        "table": (table, table_v),
        "place": (place, place_v),
        "qkv": (qkv_fine, qkv_v),
        "sf": (scale_fine, sf_s),
        "out": (out_fine, out_v),
        "gf": (gain_ffn, gf_v),
        "fin": (ffn_in, fin_v),
        "fout": (ffn_out, fout_v),
        "up": (up_proj, up_v),
        "gc": (gain_coarse, gc_v),
        "sc": (scale_coarse, sc_s),
        "qkvc": (qkv_coarse, qkvc_v),
        "outc": (out_coarse, outc_v),
    }
    loads = {}
    for i, name in list(enumerate(names)) + list(enumerate(again)):
        loads[name] = pltpu.make_async_copy(*pairs[name], local_sem.at[i])
    for name in names[:4]:
        loads[name].start()
    ha, wa = lax.axis_index("ha"), lax.axis_index("wa")
    core = lax.rem(ha, 2)
    x = lax.div(ha, 4)
    z = lax.div(wa, 2)
    y = lax.rem(lax.div(ha, 2), 2) * 2 + lax.rem(wa, 2)

    def far(step, count):
        return min(step, count - step)

    def neighbour(i):
        side_r, side_c = PIECES[i][:2]
        return (lax.rem(ha - side_r + n_ha, n_ha), lax.rem(wa - side_c + n_wa, n_wa))

    def row_peer(d):
        to_z = lax.rem(z + d // 2, n_z)
        to_core = lax.rem(core + d % 2, 2)
        return (ha - core + to_core, wa - 2 * z + 2 * to_z)

    def tile_peer(d):
        to_x = lax.rem(x + d // 4, n_x)
        to_y = lax.rem(y + d % 4, 4)
        return (4 * to_x + 2 * lax.div(to_y, 2) + core, 2 * z + lax.rem(to_y, 2))

    hops = [(far(d // 2, n_z), row_peer, d) for d in range(1, g_row)]
    hops += [(far(d // 4, n_x) + far(d % 4, 4), tile_peer, d) for d in range(1, g_tile)]
    hops += [(3 if PIECES[i][0] else 2, neighbour, i) for i in range(len(PIECES))]
    hops.sort(key=lambda hop: -hop[0])
    barrier = pltpu.get_barrier_semaphore()
    where = {}
    for _, of, d in hops:
        where[of, d] = of(d)
        pl.semaphore_signal(barrier, inc=1, device_id=where[of, d], device_id_type=MESH)
    neighbours = [where[neighbour, i] for i in range(len(PIECES))]
    row_peers = [(d, where[of, d]) for _, of, d in hops if of is row_peer]
    tile_peers = [(d, where[of, d]) for _, of, d in hops if of is tile_peer]
    for name in names[4:]:
        loads[name].start()

    def spread(src, dst, send_sem, recv_sem, peers):
        for d, peer in peers:
            pltpu.make_async_remote_copy(
                src_ref=src,
                dst_ref=dst.at[d],
                send_sem=send_sem,
                recv_sem=recv_sem,
                device_id=peer,
                device_id_type=MESH,
            ).start()
        others = dst.at[pl.ds(1, len(peers))]
        return pltpu.make_async_remote_copy(
            src_ref=others,
            dst_ref=others,
            send_sem=send_sem,
            recv_sem=recv_sem,
            device_id=peers[0][1],
            device_id_type=MESH,
        )

    loads["tok"].wait()
    loads["ga"].wait()
    normed = rms(tok_v[...].astype(F32), ga_v[...]).astype(BF)
    loads["qkv"].wait()
    proj = dot(normed, qkv_v[...])
    loads["pick"].wait()
    for name in again:
        loads[name].start()
    same = pick_v[:, COUNT:]

    def head_norm(values):
        high, low = split(values * values)
        size = (dot(high, same) + dot(low, same)) * (1 / HD)
        return values * lax.rsqrt(size + EPS)

    key, value = head_norm(proj[:, C : 2 * C]).astype(BF), proj[:, 2 * C :].astype(BF)
    send_v[...] = dot(pick_v[:, :COUNT], jnp.concatenate([key, value], 1)).astype(BF)

    pl.semaphore_wait(barrier, len(hops))
    for i, (_, _, first, rows) in enumerate(PIECES):
        pltpu.make_async_remote_copy(
            src_ref=send_v.at[pl.ds(first, rows)],
            dst_ref=halo_v.at[pl.ds(first, rows)],
            send_sem=halo_send,
            recv_sem=halo_recv,
            device_id=neighbours[i],
            device_id_type=MESH,
        ).start()
    halos = pltpu.make_async_remote_copy(
        src_ref=send_v,
        dst_ref=halo_v,
        send_sem=halo_send,
        recv_sem=halo_recv,
        device_id=neighbours[0],
        device_id_type=MESH,
    )

    loads["table"].wait()
    loads["place"].wait()
    loads["sf"].wait()
    perm = table_v[:, :COUNT]
    tok_p[...] = dot(perm, tok_v[...]).astype(BF)
    lane_head = lax.broadcasted_iota(jnp.int32, (COUNT, C), 1) // HD
    scales = jnp.zeros((1, C), F32)
    for h in range(HEADS):
        scales = jnp.where(lane_head[0:1] == h, sf_s[h] * (LOG2E / HD), scales)
    query = dot(perm, (head_norm(proj[:, :C]) * scales).astype(BF)).astype(BF)
    zero, one = jnp.zeros((COUNT, C), BF), jnp.ones((COUNT, C), BF)
    queries = [jnp.where(lane_head == h, query, zero) for h in range(HEADS)]

    key_row = place_v[0:1, :] + ha * SIDE
    key_col = place_v[1:2, :] + wa * SIDE
    inside = (
        (key_row >= 0) & (key_row < SIDE * n_ha) & (key_col >= 0) & (key_col < SIDE * n_wa)
    ).astype(F32)
    mask_v[...] = table_v[:EDGE, 3 * COUNT : 4 * COUNT].astype(F32) * inside

    def attend(rows, keys, value, mask):
        sums = [0.0, 0.0]
        for h in range(HEADS):
            raw = dot_t(queries[h][:rows], keys)
            weights = (jnp.exp2(raw) * mask).astype(BF)
            count = jnp.where(lane_head == h + 1 - 2 * (h % 2), one, zero)
            sums[h % 2] += dot(weights, jnp.where(lane_head == h, value, count))
        return sums

    def finished(sum_a, sum_b, tok):
        even = lax.rem(lane_head[: tok.shape[0]], 2) == 0
        over = jnp.where(even, sum_a, sum_b)
        under = jnp.where(even, sum_b, sum_a)
        under = jnp.concatenate(
            [pltpu.roll(under[:, :LANES], HD, 1), pltpu.roll(under[:, LANES:], HD, 1)], 1
        )
        attn = (over / under).astype(BF)
        h1 = (tok.astype(F32) + dot(attn, out_v[...])).astype(BF)
        h1 = h1.astype(F32)
        n2 = rms(h1, gf_v[...]).astype(BF)
        acc = 0.0
        for part in range(FFH // C):
            gate = dot(n2, fin_v[:, part * C : (part + 1) * C])
            lift = dot(n2, fin_v[:, FFH + part * C : FFH + (part + 1) * C])
            bend = jnp.tanh(gate * (GELU + (GELU * 0.044715) * (gate * gate)))
            gated = (gate * lift * (1.0 + bend)).astype(BF)
            acc = acc + dot(gated, fout_v[part * C : (part + 1) * C, :])
        return (h1 + 0.5 * acc).astype(BF)

    own_mask = table_v[:, 2 * COUNT : 3 * COUNT].astype(F32)
    sum_a, sum_b = attend(COUNT, key, value, own_mask)
    own_v[0] = sum_a[:EDGE]
    own_v[1] = sum_b[:EDGE]
    for name in ("out", "gf", "fin", "fout"):
        loads[name].wait()
    fine = finished(sum_a[EDGE:], sum_b[EDGE:], tok_p[EDGE:, :])
    fine_v[EDGE:, :] = fine
    part_v[...] = jnp.sum(fine.astype(F32), 0, keepdims=True)

    for name in ("up", "gc", "qkvc"):
        loads[name].wait()
    up_high, up_low = split(up_v[...].astype(F32) * gc_v[...])

    def through(part):
        after = qkvc_v[:, part * CC : (part + 1) * CC]
        return (dot(up_high, after) + dot(up_low, after)).astype(BF)

    key_m[...] = through(1)

    halos.wait_recv()
    sum_a, sum_b = attend(EDGE, halo_v[:, :C], halo_v[:, C:], mask_v[...])
    fine = finished(own_v[0] + sum_a, own_v[1] + sum_b, tok_p[:EDGE, :])
    fine_v[:EDGE, :] = fine
    pooled = part_v[...] + jnp.sum(fine.astype(F32), 0, keepdims=True)
    pooled = (pooled * (1 / COUNT)).astype(BF)

    row = pooled.astype(F32)
    loads["sc"].wait()
    own = jnp.broadcast_to(row, (HEADS_C, C)).astype(BF)
    coarse_own = dot(own, up_v[...]).astype(BF)
    coarse_f = coarse_own.astype(F32)
    factor = lax.rsqrt(jnp.mean(coarse_f * coarse_f, -1, keepdims=True) + EPS)
    head_of_row = lax.broadcasted_iota(jnp.int32, (HEADS_C, CC), 0)
    diag = head_of_row == lax.broadcasted_iota(jnp.int32, (HEADS_C, CC), 1) // HD

    def norm_of(values):
        return lax.rsqrt(jnp.sum(values * values, -1, keepdims=True) * (1 / HD) + EPS)

    ck = jnp.where(diag, dot(own, key_m[...]), 0.0) * factor
    slot = lax.broadcasted_iota(jnp.int32, (HEADS_C, LANES), 0)
    lane = lax.broadcasted_iota(jnp.int32, (HEADS_C, LANES), 1)
    scales = jnp.zeros((HEADS_C, 1), F32)
    for h in range(HEADS_C):
        scales = jnp.where(slot[:, 0:1] == h, sc_s[h] * (LOG2E / HD), scales)
    norms = norm_of(ck) * factor * scales
    twice = lax.rem(lane, LANES // 2)
    norms = jnp.sum(jnp.where(slot == twice, norms, 0.0), 0, keepdims=True)
    norms = jnp.where(twice[0:1] == HEADS_C, factor[0:1], norms)
    high, low = split(norms)
    norms = jnp.where(lane[0:1] < LANES // 2, high.astype(F32), low.astype(F32))
    row = jnp.concatenate([row, norms], 1)

    row_v[...] = row
    rows = spread(row_v, rows_v, row_send, row_recv, row_peers)
    fine_o[...] = dot(table_v[:, COUNT : 2 * COUNT], fine_v[...]).astype(BF)

    nc_own = (coarse_f * factor * gc_v[...]).astype(BF)
    cq = jnp.where(diag, dot(nc_own, qkvc_v[:, :CC]), 0.0)
    cq = (cq * norm_of(cq)).astype(BF)

    back = jnp.concatenate(split(dot_t(cq, key_m[...])), 1)

    rows.wait_recv()
    at = lax.broadcasted_iota(jnp.int32, (g_row, C + LANES), 0)
    tile = jnp.broadcast_to(row, (g_row, C + LANES))
    for d in range(1, g_row):
        tile = jnp.where(at == d, rows_v[d], tile)
    tile = tile.astype(BF)
    tile_v[...] = tile
    tiles = spread(tile_v, tiles_v, tile_send, tile_recv, tile_peers)
    tiles_v[0] = tile

    value_m[...] = through(2)

    tiles.wait_recv()
    every = tiles_v[...].reshape(g_tile * g_row, C + LANES)
    norms = every[:, C:].astype(F32).T
    norms = norms[: LANES // 2] + norms[LANES // 2 :]
    every = every[:, :C]
    scores = dot_t(back, jnp.concatenate([every, every], 1))
    cexp = jnp.exp2(scores * norms[:HEADS_C])
    rest = 1 / jnp.sum(cexp, -1, keepdims=True)
    cexp = cexp * norms[HEADS_C : HEADS_C + 1]
    mixed = dot(jnp.concatenate(split(cexp), 0), every)
    mixed = (mixed[:HEADS_C] + mixed[HEADS_C:]) * rest
    mixed = dot(jnp.concatenate(split(mixed), 0), value_m[...])
    cattn = jnp.where(diag, mixed[:HEADS_C] + mixed[HEADS_C:], 0.0)
    cattn = jnp.sum(cattn, 0, keepdims=True)
    loads["outc"].wait()
    cattn = jnp.broadcast_to(cattn, (HEADS_C, CC)).astype(BF)
    result = coarse_f
    for first in range(0, CC, C):
        result = result + dot(cattn[:, first : first + C], outc_v[first : first + C, :])
    coarse_o[...] = result[0:1].astype(BF)

    for copy in (halos, rows, tiles):
        copy.wait_send()


def finish(fine, coarse, fine_o, coarse_o, sem):
    copies = [
        pltpu.make_async_copy(fine, fine_o, sem.at[0]),
        pltpu.make_async_copy(coarse, coarse_o, sem.at[1]),
    ]
    for copy in copies:
        copy.start()
    for copy in copies:
        copy.wait()


def solution(mesh):
    sizes = (mesh.shape["ha"], mesh.shape["wa"])
    g_row, g_tile = sizes[1], sizes[0]
    pick, table, place = tables()
    pick, table = jnp.asarray(pick, BF), jnp.asarray(table, BF)
    place = jnp.asarray(place)

    def shards(
        tokens,
        gain_attn,
        qkv_fine,
        scale_fine,
        out_fine,
        gain_ffn,
        ffn_in,
        ffn_out,
        up_proj,
        gain_coarse,
        qkv_coarse,
        scale_coarse,
        out_coarse,
    ):
        hbm = pl.BlockSpec(memory_space=pl.ANY)
        fine, coarse = pl.pallas_call(
            functools.partial(kernel, sizes),
            out_shape=(pltpu.VMEM((COUNT, C), BF), pltpu.VMEM((1, CC), BF)),
            in_specs=[hbm] * 16,
            out_specs=(pl.BlockSpec(memory_space=pltpu.VMEM),) * 2,
            scratch_shapes=[
                pltpu.VMEM((COUNT, C), BF),
                pltpu.VMEM((1, C), F32),
                pltpu.VMEM((C, 3 * C), BF),
                pltpu.VMEM((C, C), BF),
                pltpu.VMEM((1, C), F32),
                pltpu.VMEM((C, 2 * FFH), BF),
                pltpu.VMEM((FFH, C), BF),
                pltpu.VMEM((C, CC), BF),
                pltpu.VMEM((1, CC), F32),
                pltpu.VMEM((CC, 3 * CC), BF),
                pltpu.VMEM((CC, CC), BF),
                pltpu.VMEM((COUNT, 2 * COUNT), BF),
                pltpu.VMEM((COUNT, 4 * COUNT), BF),
                pltpu.VMEM((8, COUNT), jnp.int32),
                pltpu.SMEM((HEADS,), F32),
                pltpu.SMEM((HEADS_C,), F32),
                pltpu.VMEM((COUNT, 2 * C), BF),
                pltpu.VMEM((COUNT, 2 * C), BF),
                pltpu.VMEM((COUNT, C), BF),
                pltpu.VMEM((2, EDGE, C), F32),
                pltpu.VMEM((EDGE, COUNT), F32),
                pltpu.VMEM((1, C), F32),
                pltpu.VMEM((COUNT, C), BF),
                pltpu.VMEM((C, CC), BF),
                pltpu.VMEM((C, CC), BF),
                pltpu.VMEM((1, C + LANES), F32),
                pltpu.VMEM((g_row, 1, C + LANES), F32),
                pltpu.VMEM((g_row, C + LANES), BF),
                pltpu.VMEM((g_tile, g_row, C + LANES), BF),
                pltpu.SemaphoreType.DMA((12,)),
                *[pltpu.SemaphoreType.DMA] * 6,
            ],
            compiler_params=pltpu.CompilerParams(
                collective_id=0, has_side_effects=True, vmem_limit_bytes=VMEM
            ),
        )(*[pltpu.with_memory_space_constraint(v, pltpu.HBM) for v in (
            tokens.reshape(COUNT, C),
            gain_attn.reshape(1, C),
            qkv_fine,
            scale_fine,
            out_fine,
            gain_ffn.reshape(1, C),
            ffn_in,
            ffn_out,
            up_proj,
            gain_coarse.reshape(1, CC),
            qkv_coarse,
            scale_coarse,
            out_coarse,
            pick,
            table,
            place,
        )])
        fine, coarse = pl.pallas_call(
            finish,
            out_shape=(
                jax.ShapeDtypeStruct((COUNT, C), BF),
                jax.ShapeDtypeStruct((1, CC), BF),
            ),
            in_specs=[pl.BlockSpec(memory_space=pltpu.VMEM)] * 2,
            out_specs=(pl.BlockSpec(memory_space=pltpu.HBM),) * 2,
            scratch_shapes=[pltpu.SemaphoreType.DMA((2,))],
            compiler_params=pltpu.CompilerParams(vmem_limit_bytes=1024 * 1024),
        )(fine, coarse)
        return fine.reshape(SIDE, SIDE, C), coarse.reshape(1, 1, CC)

    return jax.shard_map(
        shards,
        mesh=mesh,
        in_specs=(P("ha", "wa", None),) + (P(),) * 12,
        out_specs=(P("ha", "wa", None), P("ha", "wa", None)),
        check_vma=False,
    )
```
